256 devices in a mesh: shot: 16 (over y_lo, z), space: 16 (over y_hi, x, core).
Axes of the slice: x: 4, y: 4 (y_hi: 2, y_lo: 2; y = y_hi * 2 + y_lo), z: 8, core: 2. Of those that a mesh axis runs over, the one named last changes fastest.
Arguments:
- velocity: float32 [256, 128, 128], P('space'), may hold values from 2 to 6
- layer_widths: int32 [6], replicated, may hold values from 2 to 6
- forward_prev: float32 [16, 256, 128, 128], P('shot', 'space'), may hold values from -6 to 6
- forward_now: float32 [16, 256, 128, 128], P('shot', 'space'), may hold values from -6 to 6
- adjoint_now: float32 [16, 256, 128, 128], P('shot', 'space'), may hold values from -6 to 6
- adjoint_later: float32 [16, 256, 128, 128], P('shot', 'space'), may hold values from -6 to 6
- source_cell: int32 [16, 3], P('shot'), may hold values from 0 to 255, as said below
- wavelet: float32 [16, 6], P('shot'), may hold values from -40 to 40
- receiver_cells: int32 [16, 3, 2048], P('shot'), may hold values from 0 to 255, as said below
- residuals: float32 [16, 6, 2048], P('shot'), may hold values from -40 to 40
Outputs:
- forward_last: float32 [16, 256, 128, 128], P('shot', 'space')
- adjoint_first: float32 [16, 256, 128, 128], P('shot', 'space')
- gradient: float32 [256, 128, 128], P('space', 'shot')
The draws below stay inside these ranges and needn't reach their ends.
Inputs may be any that keep to these rules, and one draw needn't show every extreme that they name: `source_cell`: each shot's source is a cell of the grid, given as x, y, z indices below 256, 128, 128. `receiver_cells`: each receiver is a cell of the grid, given as x, y, z indices below 256, 128, 128; several receivers may share a cell.
All inputs are finite; a program needn't handle non-finite values.
Results may differ from the reference program's by a relative error of at most 0.0003.
Values sent between devices are 32-bit elements; how exact they have to be, the bound alone decides.
No kernel may reach another device: no remote copies, remote signals or barrier semaphores. Data moves between devices by JAX's collectives and lax.ppermute only.
A program may use at most 128 MiB of HBM per device.

```python
import jax
import jax.numpy as jnp
from jax import lax

NY = 128
NZ = 128
NREC = 2048
NT = 6
NX = 256
SHOTS = 16


def draw_source_cell(key, part):
    keys = jax.random.split(jax.random.fold_in(key, 11), 3)
    along_x = jax.random.randint(keys[0], (SHOTS,), 0, NX)
    along_y = jax.random.randint(keys[1], (SHOTS,), 0, NY)
    along_z = jax.random.randint(keys[2], (SHOTS,), 0, NZ)
    cells = jnp.stack([along_x, along_y, along_z], axis=1)
    corner = jnp.array([NX - 1, NY - 1, NZ - 1], jnp.int32)
    cells = cells.at[0].set(jnp.zeros((3,), jnp.int32)).at[SHOTS - 1].set(corner)
    return cells.astype(jnp.int32)


def draw_receiver_cells(key, part):
    keys = jax.random.split(jax.random.fold_in(key, 23), 3)
    along_x = jax.random.randint(keys[0], (SHOTS, NREC), 0, NX)
    along_y = jax.random.randint(keys[1], (SHOTS, NREC), 0, NY)
    along_z = jax.random.randint(keys[2], (SHOTS, NREC), 0, NZ)
    along_x = along_x.at[:, 0].set(0).at[:, 1].set(NX - 1)
    along_y = along_y.at[:, 0].set(0).at[:, 1].set(NY - 1)
    along_z = along_z.at[:, 0].set(0).at[:, 1].set(NZ - 1)
    return jnp.stack([along_x, along_y, along_z], axis=1).astype(jnp.int32)


def plant(drawn, key, least, top_value):
    extent = drawn.shape
    spot = [jax.random.randint(jax.random.fold_in(key, axis), (), 0, extent[axis]) for axis in range(len(extent))]
    drawn = drawn.at[tuple(spot)].set(least)
    longest = extent.index(max(extent))
    spot[longest] = (spot[longest] + 1) % extent[longest]
    return drawn.at[tuple(spot)].set(top_value)


def shard_levels(rng, extent, shards, least, top_value):
    gain, own = 1.0, jax.random.fold_in(rng, 6)
    for axis_at, parts in shards:
        heights = jnp.exp(jax.random.uniform(jax.random.fold_in(own, axis_at), (parts,), jnp.float32, least / len(shards), top_value / len(shards)))
        gain = gain * jnp.repeat(heights, extent[axis_at] // parts).reshape([-1 if axis == axis_at else 1 for axis in range(len(extent))])
    return gain


def centred(key, shape, scale, limit, cuts=(), kind=jnp.bfloat16):
    loudness = shard_levels(key, shape, cuts, -0.22, 0.18) if cuts else 1.0
    drawn = jax.random.normal(key, shape, jnp.float32) * scale * loudness
    return jnp.minimum(jnp.maximum(drawn, -limit), limit).astype(kind)


def setup_inputs(seed: int = 0) -> dict:
    splits = jax.random.split(jax.random.key(seed), 11)
    velocity = jnp.clip(2.0 + 4.0 * jax.random.uniform(splits[0], (NX, NY, NZ), jnp.float32) ** shard_levels(splits[0], (NX, NY, NZ), ((0, 16),), -0.2, 0.2), 2.0, 6.0)
    layer_widths = plant(jax.random.randint(splits[1], (6,), 2, 7), jax.random.fold_in(splits[1], 1), 2, 6).astype(jnp.int32)
    forward_prev = centred(splits[2], (SHOTS, NX, NY, NZ), 1.0, 6.0, ((0, 16), (1, 16)), jnp.float32)
    forward_now = centred(splits[3], (SHOTS, NX, NY, NZ), 1.0, 6.0, ((0, 16), (1, 16)), jnp.float32)
    adjoint_now = centred(splits[4], (SHOTS, NX, NY, NZ), 1.0, 6.0, ((0, 16), (1, 16)), jnp.float32)
    adjoint_later = centred(splits[5], (SHOTS, NX, NY, NZ), 1.0, 6.0, ((0, 16), (1, 16)), jnp.float32)
    source_cell = draw_source_cell(jax.random.fold_in(splits[10], 71), 0)
    wavelet = centred(splits[7], (SHOTS, NT), 10.0, 40.0, ((0, 16),), jnp.float32)
    receiver_cells = draw_receiver_cells(jax.random.fold_in(splits[10], 71), 0)
    residuals = centred(splits[9], (SHOTS, NT, NREC), 10.0, 40.0, ((0, 16),), jnp.float32)
    return {"velocity": velocity, "layer_widths": layer_widths, "forward_prev": forward_prev, "forward_now": forward_now, "adjoint_now": adjoint_now, "adjoint_later": adjoint_later, "source_cell": source_cell, "wavelet": wavelet, "receiver_cells": receiver_cells, "residuals": residuals}


STENCIL_COEFFS = (-205.0 / 72.0, 8.0 / 5.0, -1.0 / 5.0, 8.0 / 315.0, -1.0 / 560.0)
DT_OVER_H = 0.07
DAMPING_RATE = 0.15


def laplace_full(field):
    extent_x, extent_y, extent_z = field.shape
    padded = jnp.pad(field, 4)
    total = 3.0 * STENCIL_COEFFS[0] * field
    for offset in range(1, 5):
        beside_all = padded[4 + offset:4 + offset + extent_x, 4:4 + extent_y, 4:4 + extent_z]
        beside_all = beside_all + padded[4 - offset:4 - offset + extent_x, 4:4 + extent_y, 4:4 + extent_z]
        beside_all = beside_all + padded[4:4 + extent_x, 4 + offset:4 + offset + extent_y, 4:4 + extent_z]
        beside_all = beside_all + padded[4:4 + extent_x, 4 - offset:4 - offset + extent_y, 4:4 + extent_z]
        beside_all = beside_all + padded[4:4 + extent_x, 4:4 + extent_y, 4 + offset:4 + offset + extent_z]
        beside_all = beside_all + padded[4:4 + extent_x, 4:4 + extent_y, 4 - offset:4 - offset + extent_z]
        total = total + STENCIL_COEFFS[offset] * beside_all
    return total


def damping_full(layer_widths, extent_x, extent_y, extent_z):
    grid_x = jnp.arange(extent_x, dtype=jnp.int32)
    grid_y = jnp.arange(extent_y, dtype=jnp.int32)
    grid_z = jnp.arange(extent_z, dtype=jnp.int32)
    in_x = (grid_x < layer_widths[0]) | (grid_x >= extent_x - layer_widths[1])
    in_y = (grid_y < layer_widths[2]) | (grid_y >= extent_y - layer_widths[3])
    in_z = (grid_z < layer_widths[4]) | (grid_z >= extent_z - layer_widths[5])
    absorb = in_x[:, None, None] | in_y[None, :, None] | in_z[None, None, :]
    return jnp.where(absorb, DAMPING_RATE, 0.0).astype(jnp.float32)


def point_field(cells, amplitudes, shape):
    return jnp.zeros(shape, jnp.float32).at[cells[0], cells[1], cells[2]].add(amplitudes)


def advance_full(previous, current, weight, damping, sources):
    return (2.0 * current - (1.0 - damping) * previous + weight * (laplace_full(current) + sources)) / (1.0 + damping)


def reference(velocity, layer_widths, forward_prev, forward_now, adjoint_now, adjoint_later, source_cell, wavelet, receiver_cells, residuals):
    shape = velocity.shape
    weight = (velocity * DT_OVER_H) ** 2
    damping = damping_full(layer_widths, shape[0], shape[1], shape[2])

    def one_shot(image_total, inputs):
        first_prev, first_now, second_now, second_later, source_here, wave_here, receivers_here, residual_here = inputs
        forward_states = [first_prev, first_now]
        for step_index in range(NT):
            sources = point_field(source_here[:, None], wave_here[step_index][None], shape)
            forward_states.append(advance_full(forward_states[-2], forward_states[-1], weight, damping, sources))
        image_sum = jnp.zeros(shape, jnp.float32)
        later_state, current_state = second_later, second_now
        for level in range(NT, 0, -1):
            sources = point_field(receivers_here, residual_here[level - 1], shape)
            earlier_state = advance_full(later_state, current_state, weight, damping, sources)
            curvature = forward_states[level + 1] - 2.0 * forward_states[level] + forward_states[level - 1]
            image_sum = image_sum + earlier_state * curvature
            later_state, current_state = current_state, earlier_state
        return image_total + image_sum, (forward_states[-1], current_state)

    image_total, finals = lax.scan(one_shot, jnp.zeros(shape, jnp.float32), (forward_prev, forward_now, adjoint_now, adjoint_later, source_cell, wavelet, receiver_cells, residuals))
    return finals[0], finals[1], image_total / SHOTS
```

```python
import functools

import jax
import jax.numpy as jnp
import numpy as np
from jax import lax
from jax.experimental import pallas as pl
from jax.experimental.pallas import tpu as pltpu
from jax.sharding import PartitionSpec as P

SCALE = 5040.0
CENTRE = -43050.0
SIDE = (8064.0, -1008.0, 128.0, -9.0)
DT_OVER_H = 0.07
DAMPING_RATE = 0.15
LOAD = 256
F32, BF16 = jnp.float32, jnp.bfloat16
VMEM = pltpu.VMEM
SMEM_SPEC = pl.BlockSpec(memory_space=pltpu.SMEM)
VMEM_SPEC = pl.BlockSpec(memory_space=pltpu.VMEM)


def banded(n):
    offset = np.abs(np.arange(n)[:, None] - np.arange(n)[None, :])
    band = np.zeros((n, n), np.float32)
    for distance, coeff in enumerate(SIDE, start=1):
        band[offset == distance] = coeff
    return band


def halves(value):
    high = value.astype(BF16)
    return high, (value - high.astype(F32)).astype(BF16)


def fill_planes(scal, planes, cells_y, cells_z):
    rows = lax.broadcasted_iota(jnp.int32, (cells_y, cells_z), 0)
    lanes = lax.broadcasted_iota(jnp.int32, (cells_y, cells_z), 1)
    absorb = (rows < scal[2]) | (rows >= cells_y - scal[3]) | (lanes < scal[4]) | (lanes >= cells_z - scal[5])
    damping = jnp.where(absorb, DAMPING_RATE, 0.0).astype(F32)
    full = jnp.full((cells_y, cells_z), DAMPING_RATE, F32)
    for kind, damp in enumerate((damping, full)):
        inverse = 1.0 / (1.0 + damp)
        planes[kind, 0] = inverse
        planes[kind, 1] = 2.0 * inverse
        planes[kind, 2] = (1.0 - damp) * inverse
    planes[2] = jnp.zeros((3, cells_y, cells_z), F32)


def kind_of(scal, x, total_x):
    at = scal[6] + x
    outside = (at < 0) | (at >= total_x)
    absorbing = (at < scal[0]) | (at >= total_x - scal[1])
    return jnp.where(outside, 2, jnp.where(absorbing, 1, 0))


def substep(scal, src, prev, prev_off, weight, weight_off, planes, tz, ty, inject, store, low_x, layers, total_x, unroll):
    cells_y = src.shape[1]
    rows = 16

    def body(group, carry):
        base = group * unroll
        partial = []
        for u in range(unroll):
            high, low = halves(src[base + u + 4])
            along_z = jnp.dot(jnp.concatenate([high, low], axis=1), tz, preferred_element_type=F32)
            along_y = jnp.dot(ty, jnp.concatenate([high, low], axis=0), preferred_element_type=F32)
            partial.append(along_z + along_y)
        kinds = [kind_of(scal, low_x + base + u, total_x) for u in range(unroll)]
        for chunk in range(cells_y // rows):
            at = slice(chunk * rows, (chunk + 1) * rows)
            column = [src[base + i, at, :] for i in range(unroll + 8)]
            for u in range(unroll):
                centre = column[u + 4]
                total = partial[u][at, :] + CENTRE * centre
                for distance, coeff in enumerate(SIDE, start=1):
                    total = total + coeff * (column[u + 4 - distance] + column[u + 4 + distance])
                if inject is not None:
                    total = total + inject[base + u, at, :]
                kind = kinds[u]
                new = (
                    planes[kind, 0, at, :] * (weight[base + u + weight_off, at, :] * total)
                    + planes[kind, 1, at, :] * centre
                    - planes[kind, 2, at, :] * prev[base + u + prev_off, at, :]
                )
                store(base + u, at, new)
        return carry

    lax.fori_loop(0, layers // unroll, body, 0)


def add_source(scal, amplitude, weight, weight_off, planes, dest, dest_off, low_x, layers, total_x):
    x = scal[7] - scal[6] - low_x

    @pl.when((x >= 0) & (x < layers))
    def _():
        kind = kind_of(scal, low_x + x, total_x)
        row = pl.ds(scal[8], 1)
        lane = lax.broadcasted_iota(jnp.int32, (1, dest.shape[2]), 1)
        gain = planes[kind, 0, row, :] * weight[x + weight_off, row, :] * (SCALE * amplitude)
        dest[x + dest_off, row, :] = dest[x + dest_off, row, :] + jnp.where(lane == scal[9], gain, 0.0)


def block_kernel(first, last, forward, level, total_x, names, *refs):
    r = dict(zip(names, refs))
    scal, planes, ext = r["scal"], r["planes"], r["ext"]
    cells_y, cells_z = ext.shape[1:]
    width = ext.shape[0] - 16
    half = width // 2
    fill_planes(scal, planes, cells_y, cells_z)
    if first:
        ext[:8] = r["from_low"][:8]
        ext[8 : 8 + width] = r["own"][...]
        ext[8 + width :] = r["from_high"][:8]
        prev = r["prev"]
        prev[:4] = r["from_low"][8:12]
        prev[4 : 4 + width] = r["own_prev"][...]
        prev[4 + width :] = r["from_high"][8:12]
        if forward:
            weight = r["weight_out"]
            gain = DT_OVER_H * DT_OVER_H / SCALE
            weight[:4] = gain * r["from_low"][12:] * r["from_low"][12:]
            weight[4 : 4 + width] = gain * r["speeds"][...] * r["speeds"][...]
            weight[4 + width :] = gain * r["from_high"][12:] * r["from_high"][12:]
        else:
            weight = r["weight"]
    else:
        ext[:8] = r["from_low"][...]
        ext[8 : 8 + half] = r["own_low"][...]
        ext[8 + half : 8 + width] = r["own_high"][...]
        ext[8 + width :] = r["from_high"][...]
        prev, weight = r["prev"], r["weight"]
    tz, ty = r["tz"][...], r["ty"][...]
    middle = r["middle"]

    def store_middle(x, at, new):
        middle[x, at, :] = new

    substep(scal, ext, prev, 0, weight, 0, planes, tz, ty, None if forward else r["inject_a"], store_middle, -4, width + 8, total_x, 4)
    if forward:
        add_source(scal, r["wave"][0, level], weight, 0, planes, middle, 0, -4, width + 8, total_x)

    final = r["final"]

    def store_final(x, at, new):
        final[x, at, :] = new

    inject = None if forward else r["inject_b"].at[pl.ds(4, width)]
    substep(scal, middle, ext, 8, weight, 4, planes, tz, ty, inject, store_final, 0, width, total_x, 4)
    if forward:
        add_source(scal, r["wave"][0, level + 1], weight, 4, planes, final, 0, 0, width, total_x)
    if not last:
        r["out_low"][...] = final[:half]
        r["out_high"][...] = final[half:]


def place_kernel(low_off, scal, cells, values, *refs):
    outs, (counts, table) = refs[:-2], refs[-2:]
    layers, cells_y, cells_z = outs[0].shape
    steps, receivers = values.shape
    groups = receivers // 128
    x = cells[0:1, :] - scal[6] + low_off
    inside = (x >= 0) & (x < layers)
    key = jnp.where(inside, x * cells_y + cells[1:2, :], -1)
    flag = jnp.where(inside, 1.0, 0.0).astype(F32)
    flag_rows = jnp.concatenate([flag[:, g * 128 : (g + 1) * 128] for g in range(groups)], axis=0)
    r0 = lax.broadcasted_iota(jnp.int32, (128, 128), 0)
    r1 = lax.broadcasted_iota(jnp.int32, (128, 128), 1)
    upper = jnp.where(r0 <= r1, 1.0, 0.0).astype(BF16)
    within = jnp.dot(flag_rows.astype(BF16), upper, preferred_element_type=F32)
    g0 = lax.broadcasted_iota(jnp.int32, (groups, groups), 0)
    g1 = lax.broadcasted_iota(jnp.int32, (groups, groups), 1)
    before = jnp.where(g1 < g0, 1.0, 0.0).astype(BF16)
    totals = jnp.broadcast_to(within[:, 127:128], (groups, 128)).astype(BF16)
    rank = within - flag_rows + jnp.dot(before, totals, preferred_element_type=F32)
    rank = jnp.where(flag_rows > 0.0, rank, -1.0)
    for g in range(groups):
        counts[0:1, g * 128 : (g + 1) * 128] = rank[g : g + 1, :]
    number = jnp.sum(flag).astype(jnp.int32)
    table[...] = jnp.zeros(table.shape, BF16)
    high_key = key // 128
    parts = [high_key.astype(F32), (key - high_key * 128).astype(F32), cells[2:3, :].astype(F32)]
    table[0:16] = jnp.concatenate(parts + [jnp.zeros((13, receivers), F32)], axis=0).astype(BF16)
    scaled = values[...] * SCALE
    high = scaled.astype(BF16)
    rest = scaled - high.astype(F32)
    mid = rest.astype(BF16)
    pad = jnp.zeros((16 - steps, receivers), F32)
    table[16:32] = jnp.concatenate([high.astype(F32), pad], axis=0).astype(BF16)
    table[32:48] = jnp.concatenate([mid.astype(F32), pad], axis=0).astype(BF16)

    def one_load(load, carry):
        slot = lax.broadcasted_iota(jnp.int32, (LOAD, receivers), 0) + load * LOAD
        pick = jnp.where(slot == counts[0:1, :].astype(jnp.int32), 1.0, 0.0).astype(BF16)
        nt = (((1,), (1,)), ((), ()))
        picked = lax.dot_general(table[...], pick, nt, preferred_element_type=F32)
        column = lax.dot_general(pick, table[...], nt, preferred_element_type=F32)
        filled = (lax.broadcasted_iota(jnp.int32, (1, LOAD), 1) + load * LOAD) < number
        spot = (picked[0:1] * 128.0 + picked[1:2]).astype(jnp.int32)
        spot = jnp.where(filled, spot, -1)
        lane = lax.broadcasted_iota(jnp.int32, (LOAD, cells_z), 1)
        at_z = lane == column[:, 2:3].astype(jnp.int32)
        right_high = jnp.concatenate([jnp.where(at_z, column[:, 16 + s : 17 + s], 0.0) for s in range(steps)], axis=1).astype(BF16)
        right_mid = jnp.concatenate([jnp.where(at_z, column[:, 32 + s : 33 + s], 0.0) for s in range(steps)], axis=1).astype(BF16)

        def one_layer(layer, c):
            row = lax.broadcasted_iota(jnp.int32, (cells_y, LOAD), 0) + layer * cells_y
            left = jnp.where(row == spot, 1.0, 0.0).astype(BF16)
            placed = jnp.dot(left, right_high, preferred_element_type=F32)
            placed = placed + jnp.dot(left, right_mid, preferred_element_type=F32)

            @pl.when(load == 0)
            def _():
                for s in range(steps):
                    outs[s][layer] = placed[:, s * cells_z : (s + 1) * cells_z]

            @pl.when(load > 0)
            def _():
                for s in range(steps):
                    outs[s][layer] = outs[s][layer] + placed[:, s * cells_z : (s + 1) * cells_z]

            return c

        lax.fori_loop(0, layers, one_layer, 0)
        return carry

    lax.fori_loop(0, jnp.maximum((number + LOAD - 1) // LOAD, 1), one_load, 0)


def image_kernel(me_ref, count, *refs):
    fields, outs = refs[:14], refs[14:]
    f, a = fields[:8], fields[8:]
    me = me_ref[0]
    low_bit, top_bit = me & 1, me >> 3
    half = outs[0].shape[1]

    def piece(x0, chunk):
        rows = pl.ds(pl.multiple_of(chunk * 8, 8), 8)

        def read(ref):
            off = (ref.shape[0] - 2 * half) // 2
            return ref[off + x0 : off + x0 + half, rows, :]

        f_values = [read(ref) for ref in f]
        slopes = [f_values[i + 1] - f_values[i] for i in range(7)]
        total = read(a[0]) * (slopes[1] - slopes[0])
        for n in range(1, 6):
            total = total + read(a[n]) * (slopes[n + 1] - slopes[n])
        return total * (1.0 / count)

    def body(j, carry):
        for which in range(2):
            outs[which][j] = piece(0, (top_bit ^ which) * 8 + j)
            outs[2 + which][j] = piece(half, j * 2 + (low_bit ^ which))
        return carry

    lax.fori_loop(0, 8, body, 0)


def call(kernel, out_shapes, inputs, scratch=(), smem=1, cost=(0, 0), name=None):
    vmem_inputs = [x for x in inputs[smem:]]
    return pl.pallas_call(
        kernel,
        out_shape=out_shapes,
        in_specs=[SMEM_SPEC] * smem + [VMEM_SPEC] * len(vmem_inputs),
        out_specs=[VMEM_SPEC] * len(out_shapes),
        scratch_shapes=list(scratch),
        compiler_params=pltpu.CompilerParams(vmem_limit_bytes=VLIM),
        cost_estimate=pl.CostEstimate(flops=cost[0], bytes_accessed=cost[1], transcendentals=0),
        name=name,
    )(*inputs[:smem], *vmem_inputs)


VLIM = 48 * 1024 * 1024


def per_device(velocity, layer_widths, forward_prev, forward_now, adjoint_now, adjoint_later, source_cell, wavelet, receiver_cells, residuals):
    width, cells_y, cells_z = velocity.shape
    total_x = width * lax.axis_size("space")
    start_x = lax.axis_index("space") * width
    shots = lax.axis_size("shot")
    steps = wavelet.shape[1]
    half = width // 2
    me = lax.axis_index("shot").astype(jnp.int32)
    scal = jnp.concatenate([layer_widths, start_x.astype(jnp.int32)[None], source_cell[0]])
    band = banded(cells_z)
    tz = jnp.asarray(np.concatenate([band, band], axis=0), BF16)
    ty = jnp.asarray(np.concatenate([banded(cells_y)] * 2, axis=1), BF16)
    sds = lambda n: jax.ShapeDtypeStruct((n, cells_y, cells_z), F32)
    count = lax.axis_size("space")
    up = [(i, i + 1) for i in range(count - 1)]
    down = [(b, a) for a, b in up]

    def exchange(to_low, to_high):
        return lax.ppermute(to_high, "space", up), lax.ppermute(to_low, "space", down)

    fp, fn, an, al = forward_prev[0], forward_now[0], adjoint_now[0], adjoint_later[0]
    f_in = exchange(
        jnp.concatenate([fn[:half], fp[:4], velocity[:4]]),
        jnp.concatenate([fn[half:], fp[width - 4 :], velocity[width - 4 :]]),
    )
    a_in = exchange(
        jnp.concatenate([an[:half], al[:4]]),
        jnp.concatenate([an[half:], al[width - 4 :]]),
    )
    sources = call(
        functools.partial(place_kernel, 4),
        [sds(width + 8)] * steps,
        [scal, receiver_cells[0], residuals[0]],
        [pltpu.VMEM((1, residuals.shape[2]), F32), pltpu.VMEM((48, residuals.shape[2]), BF16)],
        name="place_receivers",
    )
    planes = pltpu.VMEM((3, 3, cells_y, cells_z), F32)
    ext = pltpu.VMEM((width + 16, cells_y, cells_z), F32)
    prev_scratch = pltpu.VMEM((width + 8, cells_y, cells_z), F32)
    final_scratch = pltpu.VMEM((width, cells_y, cells_z), F32)

    def block(first, last, forward, level, inputs):
        names = [n for n, _ in inputs]
        outs, out_names = [sds(width + 8)], ["middle"]
        if first and forward:
            outs.append(sds(width + 8))
            out_names.append("weight_out")
        scratch, scratch_names = [planes, ext], ["planes", "ext"]
        if first:
            scratch.append(prev_scratch)
            scratch_names.append("prev")
        if last:
            outs.append(sds(width))
            out_names.append("final")
        else:
            outs += [sds(half)] * 2
            out_names += ["out_low", "out_high"]
        outs_names_scratch = list(scratch_names)
        if not last:
            scratch.append(final_scratch)
            outs_names_scratch.append("final")
        smem = 2 if forward else 1
        got = call(
            functools.partial(block_kernel, first, last, forward, level, total_x, names + out_names + outs_names_scratch),
            outs,
            [v for _, v in inputs],
            scratch,
            smem,
            name=("forward" if forward else "adjoint") + "_block",
        )
        return dict(zip(out_names, got))

    tables = [("tz", tz), ("ty", ty)]
    f0 = block(True, False, True, 0, [("scal", scal), ("wave", wavelet), ("from_low", f_in[0]), ("own", fn), ("from_high", f_in[1]), ("own_prev", fp), ("speeds", velocity)] + tables)
    weight = f0["weight_out"]
    f_in = exchange(f0["out_low"], f0["out_high"])
    a0 = block(True, False, False, 0, [("scal", scal), ("from_low", a_in[0]), ("own", an), ("from_high", a_in[1]), ("own_prev", al), ("weight", weight), ("inject_a", sources[5]), ("inject_b", sources[4])] + tables)
    a_in = exchange(a0["out_low"], a0["out_high"])

    def later(last, forward, level, before, arrived, extra):
        head = [("scal", scal)] + ([("wave", wavelet)] if forward else [])
        return block(False, last, forward, level, head + [("from_low", arrived[0]), ("own_low", before["out_low"]), ("own_high", before["out_high"]), ("from_high", arrived[1]), ("prev", before["middle"]), ("weight", weight)] + extra + tables)

    f1 = later(False, True, 2, f0, f_in, [])
    f_in = exchange(f1["out_low"], f1["out_high"])
    a1 = later(False, False, 0, a0, a_in, [("inject_a", sources[3]), ("inject_b", sources[2])])
    a_in = exchange(a1["out_low"], a1["out_high"])
    f2 = later(True, True, 4, f1, f_in, [])
    a2 = later(True, False, 0, a1, a_in, [("inject_a", sources[1]), ("inject_b", sources[0])])

    whole = lambda d: jnp.concatenate([d["out_low"], d["out_high"]])
    f_all = [fp, fn, f0["middle"], whole(f0), f1["middle"], whole(f1), f2["middle"], f2["final"]]
    a_all = [a2["final"], a2["middle"], whole(a1), a1["middle"], whole(a0), a0["middle"]]
    part = jax.ShapeDtypeStruct((8, half, 8, cells_z), F32)
    keep_a, send_a, keep_b, send_b = call(
        functools.partial(lambda c, m, *refs: image_kernel(m, c, *refs), shots),
        [part] * 4,
        [me[None]] + f_all + a_all,
        name="image",
    )
    gradient = reduce_shots(me, keep_a, send_a, keep_b, send_b)
    return f2["final"][None], a2["final"][None], gradient


def flip(value, bit):
    return lax.ppermute(value, "shot", [(i, i ^ bit) for i in range(lax.axis_size("shot"))])


def reduce_shots(me, keep_a, send_a, keep_b, send_b):
    got_a, got_b = flip(send_a, 8), flip(send_b, 1)
    low_bit, top_bit = me & 1, me >> 3
    mid = (me >> 1) & 3
    half = keep_a.shape[1:]
    pick = lambda v, axis, i: lax.dynamic_index_in_dim(v, i, axis, keepdims=False)
    ka, ga = (v.reshape((4, 2) + half) for v in (keep_a, got_a))
    kb, gb = (v.reshape((2, 4) + half) for v in (keep_b, got_b))
    sa = pick(ka, 1, 1 - low_bit) + pick(ga, 1, 1 - low_bit)
    sb = pick(kb, 0, 1 - top_bit) + pick(gb, 0, 1 - top_bit)
    ra, rb = flip(sa, 1), flip(sb, 8)
    wa = pick(ka, 1, low_bit) + pick(ga, 1, low_bit) + ra
    wb = pick(kb, 0, top_bit) + pick(gb, 0, top_bit) + rb
    both = jnp.concatenate([wa, wb], axis=1)
    total = pick(both, 0, mid)
    for d in (1, 2, 3):
        total = total + flip(pick(both, 0, mid ^ d), 2 * d)
    return total


def solution(mesh):
    placed = (
        P("space", None, None),
        P(),
        P("shot", "space", None, None),
        P("shot", "space", None, None),
        P("shot", "space", None, None),
        P("shot", "space", None, None),
        P("shot", None),
        P("shot", None),
        P("shot", None, None),
        P("shot", None, None),
    )
    return jax.shard_map(
        per_device,
        mesh=mesh,
        in_specs=placed,
        out_specs=(P("shot", "space", None, None), P("shot", "space", None, None), P("space", "shot", None)),
        check_vma=False,
    )
```

```python
import functools

import jax
import jax.numpy as jnp
import numpy as np
from jax import lax
from jax.experimental import pallas as pl
from jax.experimental.pallas import tpu as pltpu
from jax.sharding import PartitionSpec as P

SCALE = 5040.0
CENTRE = -43050.0
SIDE = (8064.0, -1008.0, 128.0, -9.0)
DT_OVER_H = 0.07
DAMPING_RATE = 0.15
BATCH = 8
LOAD = 256
F32, BF16 = jnp.float32, jnp.bfloat16
VMEM = pltpu.VMEM
SMEM_SPEC = pl.BlockSpec(memory_space=pltpu.SMEM)
VMEM_SPEC = pl.BlockSpec(memory_space=pltpu.VMEM)


def banded(n):
    offset = np.abs(np.arange(n)[:, None] - np.arange(n)[None, :])
    band = np.zeros((n, n), np.float32)
    for distance, coeff in enumerate(SIDE, start=1):
        band[offset == distance] = coeff
    return band


def halves(value):
    high = value.astype(BF16)
    return high, (value - high.astype(F32)).astype(BF16)


def fill_planes(scal, planes, cells_y, cells_z):
    rows = lax.broadcasted_iota(jnp.int32, (cells_y, cells_z), 0)
    lanes = lax.broadcasted_iota(jnp.int32, (cells_y, cells_z), 1)
    absorb = (rows < scal[2]) | (rows >= cells_y - scal[3]) | (lanes < scal[4]) | (lanes >= cells_z - scal[5])
    damping = jnp.where(absorb, DAMPING_RATE, 0.0).astype(F32)
    full = jnp.full((cells_y, cells_z), DAMPING_RATE, F32)
    for kind, damp in enumerate((damping, full)):
        inverse = 1.0 / (1.0 + damp)
        planes[kind, 0] = inverse
        planes[kind, 1] = 2.0 * inverse
        planes[kind, 2] = (1.0 - damp) * inverse
    planes[2] = jnp.zeros((3, cells_y, cells_z), F32)


def kind_of(scal, x, total_x):
    at = scal[6] + x
    outside = (at < 0) | (at >= total_x)
    absorbing = (at < scal[0]) | (at >= total_x - scal[1])
    return jnp.where(outside, 2, jnp.where(absorbing, 1, 0))


def right_of(table, load, level, cells_z):
    rows = pl.ds(pl.multiple_of(load * LOAD, LOAD), LOAD)
    lane = lax.broadcasted_iota(jnp.int32, (LOAD, cells_z), 1)
    at_z = lane == table[rows, 0:1].astype(jnp.int32)
    parts = [jnp.where(at_z, table[rows, 16 * p + level : 16 * p + level + 1], 0.0) for p in (1, 2)]
    return jnp.concatenate(parts, axis=1).astype(BF16)


def placed_layers(spots, load, right, first_layer, cells_y, cells_z):
    row = lax.broadcasted_iota(jnp.int32, (BATCH * cells_y, LOAD), 0) + first_layer * cells_y
    left = jnp.where(row == spots[pl.ds(load, 1), :], 1.0, 0.0).astype(BF16)
    both = jnp.dot(left, right, preferred_element_type=F32)
    return both[:, :cells_z] + both[:, cells_z:]


def substep(scal, src, prev, prev_off, weight, weight_off, planes, tz, ty, inject, dest, low_x, layers, total_x):
    cells_y, cells_z = src.shape[1:]
    rows = 16
    if inject is not None:
        spots, table, loads, level, inject_off = inject
        right = right_of(table, 0, level, cells_z)

    def body(group, carry):
        base = group * BATCH
        high, low = halves(src[pl.ds(base + 4, BATCH)])
        side_by_side = jnp.concatenate([high, low], axis=2).reshape(BATCH * cells_y, 2 * cells_z)
        along_z = jnp.dot(side_by_side, tz, preferred_element_type=F32)
        stacked = jnp.concatenate(
            [jnp.concatenate([part[u] for u in range(BATCH)], axis=1) for part in (high, low)], axis=0
        )
        along_y = jnp.dot(ty, stacked, preferred_element_type=F32)
        if inject is not None:
            along_z = along_z + placed_layers(spots, 0, right, base + inject_off, cells_y, cells_z)
        partial = [
            along_z[u * cells_y : (u + 1) * cells_y] + along_y[:, u * cells_z : (u + 1) * cells_z]
            for u in range(BATCH)
        ]
        kinds = [kind_of(scal, low_x + base + u, total_x) for u in range(BATCH)]
        for chunk in range(cells_y // rows):
            at = slice(chunk * rows, (chunk + 1) * rows)
            column = [src[base + i, at, :] for i in range(BATCH + 8)]
            for u in range(BATCH):
                centre = column[u + 4]
                total = partial[u][at, :] + CENTRE * centre
                for distance, coeff in enumerate(SIDE, start=1):
                    total = total + coeff * (column[u + 4 - distance] + column[u + 4 + distance])
                kind = kinds[u]
                dest[base + u, at, :] = (
                    planes[kind, 0, at, :] * (weight[base + u + weight_off, at, :] * total)
                    + planes[kind, 1, at, :] * centre
                    - planes[kind, 2, at, :] * prev[base + u + prev_off, at, :]
                )
        return carry

    lax.fori_loop(0, layers // BATCH, body, 0)
    if inject is not None:

        def another_load(load, carry):
            more = right_of(table, load, level, cells_z)

            def some_layers(group, c):
                base = group * BATCH
                placed = placed_layers(spots, load, more, base + inject_off, cells_y, cells_z)
                for u in range(BATCH):
                    kind = kind_of(scal, low_x + base + u, total_x)
                    term = planes[kind, 0] * (weight[base + u + weight_off] * placed[u * cells_y : (u + 1) * cells_y])
                    dest[base + u] = dest[base + u] + term
                return c

            return lax.fori_loop(0, layers // BATCH, some_layers, carry)

        lax.fori_loop(1, loads[0], another_load, 0)


def add_source(scal, amplitude, weight, weight_off, planes, dest, dest_off, low_x, layers, total_x):
    x = scal[7] - scal[6] - low_x

    @pl.when((x >= 0) & (x < layers))
    def _():
        kind = kind_of(scal, low_x + x, total_x)
        row = pl.ds(scal[8], 1)
        lane = lax.broadcasted_iota(jnp.int32, (1, dest.shape[2]), 1)
        gain = planes[kind, 0, row, :] * weight[x + weight_off, row, :] * (SCALE * amplitude)
        dest[x + dest_off, row, :] = dest[x + dest_off, row, :] + jnp.where(lane == scal[9], gain, 0.0)


def block_kernel(first, last, forward, level, total_x, names, *refs):
    r = dict(zip(names, refs))
    scal, planes, ext, weight = r["scal"], r["planes"], r["ext"], r["weight"]
    width = r["own"].shape[0]
    half = width // 2
    odd = scal[10]
    low_edge, high_edge = scal[6] == 0, scal[6] + width == total_x
    at_edge = low_edge | high_edge
    halo_a, halo_b = pl.ds((1 - odd) * (8 + width), 8), pl.ds(odd * (8 + width), 8)
    ext[halo_a] = r["from_a"][:8]
    ext[halo_b] = jnp.where(at_edge, 0.0, r["from_b"][:8])
    ext[8 : 8 + width] = r["own"][...]
    if first:
        prev = r["prev"]
        thin_a, thin_b = pl.ds((1 - odd) * (4 + width), 4), pl.ds(odd * (4 + width), 4)
        prev[thin_a] = r["from_a"][8:12]
        prev[thin_b] = r["from_b"][8:12]
        prev[4 : 4 + width] = r["own_prev"][...]
        if forward:
            gain = DT_OVER_H * DT_OVER_H / SCALE
            weight[thin_a] = gain * r["from_a"][12:] * r["from_a"][12:]
            weight[thin_b] = gain * r["from_b"][12:] * r["from_b"][12:]
            weight[4 : 4 + width] = gain * r["speeds"][...] * r["speeds"][...]
    else:
        prev = r["prev"]
    tz, ty = r["tz"][...], r["ty"][...]
    middle, final = r["middle"], r["final"]
    inject = (lambda n, off: None) if forward else (lambda n, off: (r["spots"], r["table"], r["loads"], n, off))
    substep(scal, ext, prev, 0, weight, 0, planes, tz, ty, inject(level, 0), middle, -4, width + 8, total_x)
    if forward:
        add_source(scal, r["wave"][0, level], weight, 0, planes, middle, 0, -4, width + 8, total_x)
    substep(scal, middle, ext, 8, weight, 4, planes, tz, ty, inject(level - 1, 4), final, 0, width, total_x)
    if forward:
        add_source(scal, r["wave"][0, level + 1], weight, 4, planes, final, 0, 0, width, total_x)
    if not last:
        r["to_a"][...] = final[pl.ds((1 - odd) * half, half)]
        r["to_b"][...] = final[pl.ds(odd * half, half)]


def receivers_kernel(low_off, layers, cells_y, cells_z, scal, cells, values, loads, spots, table, planes, counts, entries):
    fill_planes(scal, planes, cells_y, cells_z)
    steps, receivers = values.shape
    groups = receivers // 128
    x = cells[0:1, :] - scal[6] + low_off
    inside = (x >= 0) & (x < layers)
    key = jnp.where(inside, x * cells_y + cells[1:2, :], -1)
    flag = jnp.where(inside, 1.0, 0.0).astype(F32)
    flag_rows = jnp.concatenate([flag[:, g * 128 : (g + 1) * 128] for g in range(groups)], axis=0)
    r0 = lax.broadcasted_iota(jnp.int32, (128, 128), 0)
    r1 = lax.broadcasted_iota(jnp.int32, (128, 128), 1)
    upper = jnp.where(r0 <= r1, 1.0, 0.0).astype(BF16)
    within = jnp.dot(flag_rows.astype(BF16), upper, preferred_element_type=F32)
    g0 = lax.broadcasted_iota(jnp.int32, (groups, groups), 0)
    g1 = lax.broadcasted_iota(jnp.int32, (groups, groups), 1)
    before = jnp.where(g1 < g0, 1.0, 0.0).astype(BF16)
    totals = jnp.broadcast_to(within[:, 127:128], (groups, 128)).astype(BF16)
    rank = within - flag_rows + jnp.dot(before, totals, preferred_element_type=F32)
    rank = jnp.where(flag_rows > 0.0, rank, -1.0)
    for g in range(groups):
        counts[0:1, g * 128 : (g + 1) * 128] = rank[g : g + 1, :]
    number = jnp.sum(flag).astype(jnp.int32)
    filled_loads = jnp.maximum((number + LOAD - 1) // LOAD, 1)
    loads[0] = filled_loads
    high_key = key // 128
    parts = [cells[2:3, :].astype(F32), high_key.astype(F32), (key - high_key * 128).astype(F32)]
    entries[0:16] = jnp.concatenate(parts + [jnp.zeros((13, receivers), F32)], axis=0).astype(BF16)
    scaled = values[...] * SCALE
    high = scaled.astype(BF16)
    rest = (scaled - high.astype(F32)).astype(BF16)
    pad = jnp.zeros((16 - steps, receivers), BF16)
    entries[16:32] = jnp.concatenate([high, pad], axis=0)
    entries[32:48] = jnp.concatenate([rest, pad], axis=0)
    entries[48:] = jnp.zeros((entries.shape[0] - 48, receivers), BF16)

    def one_load(load, carry):
        slot = lax.broadcasted_iota(jnp.int32, (LOAD, receivers), 0) + load * LOAD
        pick = jnp.where(slot == counts[0:1, :].astype(jnp.int32), 1.0, 0.0).astype(BF16)
        nt = (((1,), (1,)), ((), ()))
        picked = lax.dot_general(entries[0:16], pick, nt, preferred_element_type=F32)
        column = lax.dot_general(pick, entries[...], nt, preferred_element_type=F32)
        filled = (lax.broadcasted_iota(jnp.int32, (1, LOAD), 1) + load * LOAD) < number
        spot = (picked[1:2] * 128.0 + picked[2:3]).astype(jnp.int32)
        spots[pl.ds(load, 1), :] = jnp.where(filled, spot, -1)
        table[pl.ds(pl.multiple_of(load * LOAD, LOAD), LOAD), :] = column
        return carry

    lax.fori_loop(0, filled_loads, one_load, 0)


def image_kernel(me_ref, count, *refs):
    fields, outs = refs[:14], refs[14:]
    f, a = fields[:8], fields[8:]
    me = me_ref[0]
    low_bit, top_bit = me & 1, me >> 3
    half = outs[0].shape[1]

    def piece(x0, chunk):
        rows = pl.ds(pl.multiple_of(chunk * 8, 8), 8)

        def read(ref):
            off = (ref.shape[0] - 2 * half) // 2
            return ref[off + x0 : off + x0 + half, rows, :]

        f_values = [read(ref) for ref in f]
        slopes = [f_values[i + 1] - f_values[i] for i in range(7)]
        total = read(a[0]) * (slopes[1] - slopes[0])
        for n in range(1, 6):
            total = total + read(a[n]) * (slopes[n + 1] - slopes[n])
        return total * (1.0 / count)

    def body(j, carry):
        for which in range(2):
            outs[which][j] = piece(0, (top_bit ^ which) * 8 + j)
            outs[2 + which][j] = piece(half, j * 2 + (low_bit ^ which))
        return carry

    lax.fori_loop(0, 8, body, 0)


def pack_kernel(plan, width, count, scal, *refs):
    inputs, outs, sems = refs[:count], refs[count:-1], refs[-1]
    copies = []
    for out, at_high in zip(outs, (1 - scal[10], scal[10])):
        at = 0
        for array, layers in zip(inputs, plan):
            source = array.at[pl.ds(at_high * (width - layers), layers)]
            copies.append(pltpu.make_async_copy(source, out.at[pl.ds(at, layers)], sems.at[len(copies)]))
            at += layers
    for copy in copies:
        copy.start()
    for copy in copies:
        copy.wait()


def pack(scal, arrays, plan):
    out = jax.ShapeDtypeStruct((sum(plan),) + arrays[0].shape[1:], F32)
    return pl.pallas_call(
        functools.partial(pack_kernel, plan, arrays[0].shape[0], len(arrays)),
        out_shape=[out] * 2,
        in_specs=[SMEM_SPEC] + [pl.BlockSpec(memory_space=pltpu.HBM)] * len(arrays),
        out_specs=[VMEM_SPEC] * 2,
        scratch_shapes=[pltpu.SemaphoreType.DMA((2 * len(plan),))],
        compiler_params=pltpu.CompilerParams(vmem_limit_bytes=VLIM),
        cost_estimate=pl.CostEstimate(flops=0, bytes_accessed=4 << 20, transcendentals=0),
        name="pack",
    )(scal, *arrays)


def call(kernel, out_shapes, inputs, scratch=(), smem=1, cost=(0, 14 << 20), name=None, out_specs=None):
    vmem_inputs = [x for x in inputs[smem:]]
    return pl.pallas_call(
        kernel,
        out_shape=out_shapes,
        in_specs=[SMEM_SPEC] * smem + [VMEM_SPEC] * len(vmem_inputs),
        out_specs=out_specs or [VMEM_SPEC] * len(out_shapes),
        scratch_shapes=list(scratch),
        compiler_params=pltpu.CompilerParams(vmem_limit_bytes=VLIM),
        cost_estimate=pl.CostEstimate(flops=cost[0], bytes_accessed=cost[1], transcendentals=0),
        name=name,
    )(*inputs[:smem], *vmem_inputs)


VLIM = 14 * 1024 * 1024


def per_device(velocity, layer_widths, forward_prev, forward_now, adjoint_now, adjoint_later, source_cell, wavelet, receiver_cells, residuals):
    width, cells_y, cells_z = velocity.shape
    total_x = width * lax.axis_size("space")
    shots = lax.axis_size("shot")
    half = width // 2
    me = lax.axis_index("shot").astype(jnp.int32)
    place = lax.axis_index("space").astype(jnp.int32)
    scal = jnp.concatenate([layer_widths, (place * width)[None], source_cell[0], (place % 2)[None]])
    band = banded(cells_z)
    tz = jnp.asarray(np.concatenate([band, band], axis=0), BF16)
    ty = jnp.asarray(np.concatenate([banded(cells_y)] * 2, axis=1), BF16)
    sds = lambda n: jax.ShapeDtypeStruct((n, cells_y, cells_z), F32)
    count = lax.axis_size("space")
    swap_a = [(i, i ^ 1) for i in range(count)]
    swap_b = [(i, (i + (1 if i % 2 else -1)) % count) for i in range(count)]

    def exchange(to_a, to_b):
        from_b = lax.ppermute(to_b, "space", swap_b)
        return lax.ppermute(to_a, "space", swap_a), from_b

    fp, fn, an, al = forward_prev[0], forward_now[0], adjoint_now[0], adjoint_later[0]
    f_in = exchange(*pack(scal, [fn, fp, velocity], (half, 4, 4)))
    a_in = exchange(*pack(scal, [an, al], (half, 4)))
    receivers = residuals.shape[2]
    slots = receivers // LOAD
    loads, spots, table, planes = call(
        functools.partial(receivers_kernel, 4, width + 8, cells_y, cells_z),
        [
            jax.ShapeDtypeStruct((1,), jnp.int32),
            jax.ShapeDtypeStruct((slots, LOAD), jnp.int32),
            jax.ShapeDtypeStruct((receivers, 128), F32),
            jax.ShapeDtypeStruct((3, 3, cells_y, cells_z), F32),
        ],
        [scal, receiver_cells[0], residuals[0]],
        [pltpu.VMEM((1, receivers), F32), pltpu.VMEM((128, receivers), BF16)],
        name="list_receivers",
        out_specs=[SMEM_SPEC] + [VMEM_SPEC] * 3,
    )
    tables = [("planes", planes), ("tz", tz), ("ty", ty)]

    def block(first, last, forward, level, arrived, own, extra):
        inputs = [("scal", scal), ("wave", wavelet) if forward else ("loads", loads)]
        inputs += [("from_a", arrived[0]), ("from_b", arrived[1]), ("own", own)] + extra + tables
        if not forward:
            inputs += [("spots", spots), ("table", table)]
        outs, out_names = [sds(width + 8), sds(width)], ["middle", "final"]
        if first and forward:
            outs.append(sds(width + 8))
            out_names.append("weight")
        if not last:
            outs += [sds(half)] * 2
            out_names += ["to_a", "to_b"]
        scratch, scratch_names = [pltpu.VMEM((width + 16, cells_y, cells_z), F32)], ["ext"]
        if first:
            scratch.append(pltpu.VMEM((width + 8, cells_y, cells_z), F32))
            scratch_names.append("prev")
        names = [n for n, _ in inputs] + out_names + scratch_names
        got = call(
            functools.partial(block_kernel, first, last, forward, level, total_x, names),
            outs,
            [v for _, v in inputs],
            scratch,
            2,
            name=("forward" if forward else "adjoint") + "_block",
        )
        return dict(zip(out_names, got))

    def begin(forward, level, arrived, own, own_prev, extra):
        return block(True, False, forward, level, arrived, own, [("own_prev", own_prev)] + extra)

    def go_on(last, forward, level, arrived, before):
        return block(False, last, forward, level, arrived, before["final"], [("prev", before["middle"]), ("weight", weight)])

    f0 = begin(True, 0, f_in, fn, fp, [("speeds", velocity)])
    weight = f0["weight"]
    f_in = exchange(f0["to_a"], f0["to_b"])
    a0 = begin(False, 5, a_in, an, al, [("weight", weight)])
    a_in = exchange(a0["to_a"], a0["to_b"])
    f1 = go_on(False, True, 2, f_in, f0)
    f_in = exchange(f1["to_a"], f1["to_b"])
    a1 = go_on(False, False, 3, a_in, a0)
    a_in = exchange(a1["to_a"], a1["to_b"])
    f2 = go_on(True, True, 4, f_in, f1)
    a2 = go_on(True, False, 1, a_in, a1)

    f_all = [fp, fn, f0["middle"], f0["final"], f1["middle"], f1["final"], f2["middle"], f2["final"]]
    a_all = [a2["final"], a2["middle"], a1["final"], a1["middle"], a0["final"], a0["middle"]]
    part = jax.ShapeDtypeStruct((8, half, 8, cells_z), F32)
    keep_a, send_a, keep_b, send_b = call(
        functools.partial(lambda c, m, *refs: image_kernel(m, c, *refs), shots),
        [part] * 4,
        [me[None]] + f_all + a_all,
        name="image",
    )
    gradient = reduce_shots(me, keep_a, send_a, keep_b, send_b)
    return f2["final"][None], a2["final"][None], gradient


def flip(value, bit):
    return lax.ppermute(value, "shot", [(i, i ^ bit) for i in range(lax.axis_size("shot"))])


def reduce_shots(me, keep_a, send_a, keep_b, send_b):
    got_a, got_b = flip(send_a, 8), flip(send_b, 1)
    low_bit, top_bit = me & 1, me >> 3
    mid = (me >> 1) & 3
    half = keep_a.shape[1:]
    pick = lambda v, axis, i: lax.dynamic_index_in_dim(v, i, axis, keepdims=False)
    ka, ga = (v.reshape((4, 2) + half) for v in (keep_a, got_a))
    kb, gb = (v.reshape((2, 4) + half) for v in (keep_b, got_b))
    sa = pick(ka, 1, 1 - low_bit) + pick(ga, 1, 1 - low_bit)
    sb = pick(kb, 0, 1 - top_bit) + pick(gb, 0, 1 - top_bit)
    ra, rb = flip(sa, 1), flip(sb, 8)
    wa = pick(ka, 1, low_bit) + pick(ga, 1, low_bit) + ra
    wb = pick(kb, 0, top_bit) + pick(gb, 0, top_bit) + rb
    both = jnp.concatenate([wa, wb], axis=1)
    total = pick(both, 0, mid)
    for d in (1, 2, 3):
        total = total + flip(pick(both, 0, mid ^ d), 2 * d)
    return total


def solution(mesh):
    placed = (
        P("space", None, None),
        P(),
        P("shot", "space", None, None),
        P("shot", "space", None, None),
        P("shot", "space", None, None),
        P("shot", "space", None, None),
        P("shot", None),
        P("shot", None),
        P("shot", None, None),
        P("shot", None, None),
    )
    return jax.shard_map(
        per_device,
        mesh=mesh,
        in_specs=placed,
        out_specs=(P("shot", "space", None, None), P("shot", "space", None, None), P("space", "shot", None)),
        check_vma=False,
    )
```

```python
import functools

import jax
import jax.numpy as jnp
import numpy as np
from jax import lax
from jax.experimental import pallas as pl
from jax.experimental.pallas import tpu as pltpu
from jax.sharding import PartitionSpec as P

SCALE = 5040.0
CENTRE = -43050.0
SIDE = (8064.0, -1008.0, 128.0, -9.0)
DT_OVER_H = 0.07
DAMPING_RATE = 0.15
SHOTS = 16
BATCH = 8
LOAD = 256
F32, BF16 = jnp.float32, jnp.bfloat16
VMEM = pltpu.VMEM
SMEM_SPEC = pl.BlockSpec(memory_space=pltpu.SMEM)
VMEM_SPEC = pl.BlockSpec(memory_space=pltpu.VMEM)


def banded(n):
    offset = np.abs(np.arange(n)[:, None] - np.arange(n)[None, :])
    band = np.zeros((n, n), np.float32)
    for distance, coeff in enumerate(SIDE, start=1):
        band[offset == distance] = coeff
    return band


def halves(value):
    high = value.astype(BF16)
    return high, (value - high.astype(F32)).astype(BF16)


def fill_planes(scal, planes, cells_y, cells_z):
    rows = lax.broadcasted_iota(jnp.int32, (cells_y, cells_z), 0)
    lanes = lax.broadcasted_iota(jnp.int32, (cells_y, cells_z), 1)
    absorb = (rows < scal[2]) | (rows >= cells_y - scal[3]) | (lanes < scal[4]) | (lanes >= cells_z - scal[5])
    damping = jnp.where(absorb, DAMPING_RATE, 0.0).astype(F32)
    full = jnp.full((cells_y, cells_z), DAMPING_RATE, F32)
    for kind, damp in enumerate((damping, full)):
        inverse = 1.0 / (1.0 + damp)
        planes[kind, 0] = inverse
        planes[kind, 1] = 2.0 * inverse
        planes[kind, 2] = (1.0 - damp) * inverse
    planes[2] = jnp.zeros((3, cells_y, cells_z), F32)


def kind_of(scal, x, total_x):
    at = scal[6] + x
    outside = (at < 0) | (at >= total_x)
    absorbing = (at < scal[0]) | (at >= total_x - scal[1])
    return jnp.where(outside, 2, jnp.where(absorbing, 1, 0))


def right_of(table, load, level, cells_z):
    rows = pl.ds(pl.multiple_of(load * LOAD, LOAD), LOAD)
    lane = lax.broadcasted_iota(jnp.int32, (LOAD, cells_z), 1)
    at_z = lane == table[rows, 0:1].astype(jnp.int32)
    parts = [jnp.where(at_z, table[rows, 16 * p + level : 16 * p + level + 1], 0.0) for p in (1, 2)]
    return jnp.concatenate(parts, axis=1).astype(BF16)


def one_hot_rows(spots, load, first_layer, layers, cells_y):
    row = lax.broadcasted_iota(jnp.int32, (layers * cells_y, LOAD), 0) + first_layer * cells_y
    return jnp.where(row == spots[pl.ds(load, 1), :], 1.0, 0.0).astype(BF16)


def placed(left, right, cells_z):
    both = jnp.dot(left, right, preferred_element_type=F32)
    return both[:, :cells_z] + both[:, cells_z:]


def substep(scal, src, prev, prev_off, weight, weight_off, planes, tz, ty, inject, dest, low_x, layers, total_x, each=None, late=None):
    cells_y, cells_z = src.shape[1:]
    rows = 16
    if inject is not None:
        r, level, inject_off = inject

    def body(group, carry):
        base = group * BATCH
        high, low = halves(src[pl.ds(base + 4, BATCH)])
        side_by_side = jnp.concatenate([high, low], axis=2).reshape(BATCH * cells_y, 2 * cells_z)
        along_z = jnp.dot(side_by_side, tz, preferred_element_type=F32)
        stacked = jnp.concatenate(
            [jnp.concatenate([part[u] for u in range(BATCH)], axis=1) for part in (high, low)], axis=0
        )
        along_y = jnp.dot(ty, stacked, preferred_element_type=F32)
        if inject is not None:
            first_row = pl.multiple_of((base + inject_off) * cells_y, cells_y)
            along_z = along_z + placed(r["left"][pl.ds(first_row, BATCH * cells_y), :], r["rights"][level], cells_z)
        partial = [
            along_z[u * cells_y : (u + 1) * cells_y] + along_y[:, u * cells_z : (u + 1) * cells_z]
            for u in range(BATCH)
        ]
        kinds = [kind_of(scal, low_x + base + u, total_x) for u in range(BATCH)]
        for chunk in range(cells_y // rows):
            at = slice(chunk * rows, (chunk + 1) * rows)
            column = [src[base + i, at, :] for i in range(BATCH + 8)]
            for u in range(BATCH):
                centre = column[u + 4]
                total = partial[u][at, :] + CENTRE * centre
                for distance, coeff in enumerate(SIDE, start=1):
                    total = total + coeff * (column[u + 4 - distance] + column[u + 4 + distance])
                kind = kinds[u]
                before = prev[base + u + prev_off, at, :]
                new = (
                    planes[kind, 0, at, :] * (weight[base + u + weight_off, at, :] * total)
                    + planes[kind, 1, at, :] * centre
                    - planes[kind, 2, at, :] * before
                )
                dest[base + u, at, :] = new
                if each is not None:
                    each(base + u, at, new, centre, before)
        return carry

    lax.fori_loop(0, layers // BATCH, body, 0)
    if inject is not None:

        def another_load(load, carry):
            more = right_of(r["table"], load, level, cells_z)

            def one_layer(x, c):
                left = one_hot_rows(r["spots"], load, x + inject_off, 1, cells_y)
                kind = kind_of(scal, low_x + x, total_x)
                term = planes[kind, 0] * (weight[x + weight_off] * placed(left, more, cells_z))
                dest[x] = dest[x] + term
                if late is not None:
                    late(x, slice(None), term)
                return c

            return lax.fori_loop(0, layers, one_layer, carry)

        lax.fori_loop(1, r["loads"][0], another_load, 0)


def add_source(scal, amplitude, weight, weight_off, planes, dest, low_x, layers, total_x, late=None):
    x = scal[7] - scal[6] - low_x

    @pl.when((x >= 0) & (x < layers))
    def _():
        kind = kind_of(scal, low_x + x, total_x)
        row = pl.ds(scal[8], 1)
        lane = lax.broadcasted_iota(jnp.int32, (1, dest.shape[2]), 1)
        gain = planes[kind, 0, row, :] * weight[x + weight_off, row, :] * (SCALE * amplitude)
        term = jnp.where(lane == scal[9], gain, 0.0)
        dest[x, row, :] = dest[x, row, :] + term
        if late is not None:
            late(x, row, term)


def block_kernel(first, last, forward, level, total_x, names, *refs):
    r = dict(zip(names, refs))
    scal, planes, ext, weight = r["scal"], r["planes"], r["ext"], r["weight"]
    width = r["own"].shape[0]
    half = width // 2
    odd = scal[10]
    r["turn"][0] = r["after"][0]
    low_edge, high_edge = scal[6] == 0, scal[6] + width == total_x
    at_edge = low_edge | high_edge
    halo_a, halo_b = pl.ds((1 - odd) * (8 + width), 8), pl.ds(odd * (8 + width), 8)
    ext[halo_a] = r["from_a"][:8]
    ext[halo_b] = jnp.where(at_edge, 0.0, r["from_b"][:8])
    ext[8 : 8 + width] = r["own"][...]
    if first:
        prev = r["prev"]
        thin_a, thin_b = pl.ds((1 - odd) * (4 + width), 4), pl.ds(odd * (4 + width), 4)
        prev[thin_a] = r["from_a"][8:12]
        prev[thin_b] = r["from_b"][8:12]
        prev[4 : 4 + width] = r["own_prev"][...]
        if forward:
            gain = DT_OVER_H * DT_OVER_H / SCALE
            weight[thin_a] = gain * r["from_a"][12:] * r["from_a"][12:]
            weight[thin_b] = gain * r["from_b"][12:] * r["from_b"][12:]
            weight[4 : 4 + width] = gain * r["speeds"][...] * r["speeds"][...]
    else:
        prev = r["prev"]
    tz, ty = r["tz"][...], r["ty"][...]
    middle, final = r["middle"], r["final"]
    inject = (lambda n, off: None) if forward else (lambda n, off: (r, n, off))
    substep(scal, ext, prev, 0, weight, 0, planes, tz, ty, inject(level, 0), middle, -4, width + 8, total_x)
    if forward:
        add_source(scal, r["wave"][0, level], weight, 0, planes, middle, -4, width + 8, total_x)

    each = late = None
    image = r.get("image")
    if forward:

        def curvatures(x, at, new, centre, before):
            return centre - 2.0 * before + prev[x + 4, at, :], new - 2.0 * centre + before

        if last:

            def each(x, at, *states):
                early, recent = curvatures(x, at, *states)
                terms = r["adjoint_early"][x, at, :] * early + r["adjoint_recent"][x + 4, at, :] * recent
                image[x, at, :] = r["image_in"][x, at, :] + terms

            def late(x, at, term):
                image[x, at, :] = image[x, at, :] + r["adjoint_recent"][x + 4, at, :] * term

        else:

            def each(x, at, *states):
                r["curve_early"][x, at, :], r["curve_recent"][x, at, :] = curvatures(x, at, *states)

            def late(x, at, term):
                r["curve_recent"][x, at, :] = r["curve_recent"][x, at, :] + term

    elif not first:

        def each(x, at, new, centre, before):
            terms = centre * r["curve_recent"][x, at, :] + new * r["curve_early"][x, at, :]
            image[x, at, :] = r["image_in"][x, at, :] + terms if last else terms

        def late(x, at, term):
            image[x, at, :] = image[x, at, :] + term * r["curve_early"][x, at, :]

    substep(scal, middle, ext, 8, weight, 4, planes, tz, ty, inject(level - 1, 4), final, 0, width, total_x, each, late)
    if forward:
        add_source(scal, r["wave"][0, level + 1], weight, 4, planes, final, 0, width, total_x, late)
    if not last:
        r["to_a"][...] = final[pl.ds((1 - odd) * half, half)]
        r["to_b"][...] = final[pl.ds(odd * half, half)]
    elif not forward:
        low_bit, top_bit = scal[11] & 1, scal[11] >> 3
        shares = [[r["keep_low"], r["send_low"]], [r["keep_high"], r["send_high"]]]
        share = 1.0 / SHOTS

        def one_chunk(j, carry):
            for which in range(2):
                for upper, chunk in enumerate(((top_bit ^ which) * 8 + j, j * 2 + (low_bit ^ which))):
                    at = pl.ds(pl.multiple_of(chunk * 8, 8), 8)
                    shares[upper][which][j] = share * image[upper * half : (upper + 1) * half, at, :]
            return carry

        lax.fori_loop(0, 8, one_chunk, 0)


def receivers_kernel(low_off, layers, cells_y, cells_z, scal, cells, values, loads, spots, table, left, rights, planes, counts, entries):
    fill_planes(scal, planes, cells_y, cells_z)
    steps, receivers = values.shape
    groups = receivers // 128
    x = cells[0:1, :] - scal[6] + low_off
    inside = (x >= 0) & (x < layers)
    key = jnp.where(inside, x * cells_y + cells[1:2, :], -1)
    flag = jnp.where(inside, 1.0, 0.0).astype(F32)
    flag_rows = jnp.concatenate([flag[:, g * 128 : (g + 1) * 128] for g in range(groups)], axis=0)
    r0 = lax.broadcasted_iota(jnp.int32, (128, 128), 0)
    r1 = lax.broadcasted_iota(jnp.int32, (128, 128), 1)
    upper = jnp.where(r0 <= r1, 1.0, 0.0).astype(BF16)
    within = jnp.dot(flag_rows.astype(BF16), upper, preferred_element_type=F32)
    g0 = lax.broadcasted_iota(jnp.int32, (groups, groups), 0)
    g1 = lax.broadcasted_iota(jnp.int32, (groups, groups), 1)
    before = jnp.where(g1 < g0, 1.0, 0.0).astype(BF16)
    totals = jnp.broadcast_to(within[:, 127:128], (groups, 128)).astype(BF16)
    rank = within - flag_rows + jnp.dot(before, totals, preferred_element_type=F32)
    rank = jnp.where(flag_rows > 0.0, rank, -1.0)
    for g in range(groups):
        counts[0:1, g * 128 : (g + 1) * 128] = rank[g : g + 1, :]
    number = jnp.sum(flag).astype(jnp.int32)
    filled_loads = jnp.maximum((number + LOAD - 1) // LOAD, 1)
    loads[0] = filled_loads
    high_key = key // 128
    parts = [cells[2:3, :].astype(F32), high_key.astype(F32), (key - high_key * 128).astype(F32)]
    entries[0:16] = jnp.concatenate(parts + [jnp.zeros((13, receivers), F32)], axis=0).astype(BF16)
    scaled = values[...] * SCALE
    high = scaled.astype(BF16)
    rest = (scaled - high.astype(F32)).astype(BF16)
    pad = jnp.zeros((16 - steps, receivers), BF16)
    entries[16:32] = jnp.concatenate([high, pad], axis=0)
    entries[32:48] = jnp.concatenate([rest, pad], axis=0)
    entries[48:] = jnp.zeros((entries.shape[0] - 48, receivers), BF16)

    def one_load(load, carry):
        slot = lax.broadcasted_iota(jnp.int32, (LOAD, receivers), 0) + load * LOAD
        pick = jnp.where(slot == counts[0:1, :].astype(jnp.int32), 1.0, 0.0).astype(BF16)
        nt = (((1,), (1,)), ((), ()))
        picked = lax.dot_general(entries[0:16], pick, nt, preferred_element_type=F32)
        column = lax.dot_general(pick, entries[...], nt, preferred_element_type=F32)
        filled = (lax.broadcasted_iota(jnp.int32, (1, LOAD), 1) + load * LOAD) < number
        spot = (picked[1:2] * 128.0 + picked[2:3]).astype(jnp.int32)
        spots[pl.ds(load, 1), :] = jnp.where(filled, spot, -1)
        table[pl.ds(pl.multiple_of(load * LOAD, LOAD), LOAD), :] = column
        return carry

    lax.fori_loop(0, filled_loads, one_load, 0)
    for group in range(layers // BATCH):
        at = slice(group * BATCH * cells_y, (group + 1) * BATCH * cells_y)
        left[at, :] = one_hot_rows(spots, 0, group * BATCH, BATCH, cells_y)
    for step in range(steps):
        rights[step] = right_of(table, 0, step, cells_z)


def pack_kernel(plan, width, count, scal, *refs):
    inputs, outs, sems = refs[:count], refs[count:-1], refs[-1]
    copies = []
    for out, at_high in zip(outs, (1 - scal[10], scal[10])):
        at = 0
        for array, layers in zip(inputs, plan):
            source = array.at[pl.ds(at_high * (width - layers), layers)]
            copies.append(pltpu.make_async_copy(source, out.at[pl.ds(at, layers)], sems.at[len(copies)]))
            at += layers
    for copy in copies:
        copy.start()
    for copy in copies:
        copy.wait()


def pack(scal, arrays, plan):
    out = jax.ShapeDtypeStruct((sum(plan),) + arrays[0].shape[1:], F32)
    return pl.pallas_call(
        functools.partial(pack_kernel, plan, arrays[0].shape[0], len(arrays)),
        out_shape=[out] * 2,
        in_specs=[SMEM_SPEC] + [pl.BlockSpec(memory_space=pltpu.HBM)] * len(arrays),
        out_specs=[VMEM_SPEC] * 2,
        scratch_shapes=[pltpu.SemaphoreType.DMA((2 * len(plan),))],
        compiler_params=pltpu.CompilerParams(vmem_limit_bytes=VLIM),
        cost_estimate=pl.CostEstimate(flops=0, bytes_accessed=4 << 20, transcendentals=0),
        name="pack",
    )(scal, *[pltpu.with_memory_space_constraint(x, pltpu.HBM) for x in arrays])


def call(kernel, out_shapes, inputs, scratch=(), smem=1, cost=(0, 14 << 20), name=None, out_specs=None):
    vmem_inputs = [x for x in inputs[smem:]]
    return pl.pallas_call(
        kernel,
        out_shape=out_shapes,
        in_specs=[SMEM_SPEC] * smem + [VMEM_SPEC] * len(vmem_inputs),
        out_specs=out_specs or [VMEM_SPEC] * len(out_shapes),
        scratch_shapes=list(scratch),
        compiler_params=pltpu.CompilerParams(vmem_limit_bytes=VLIM),
        cost_estimate=pl.CostEstimate(flops=cost[0], bytes_accessed=cost[1], transcendentals=0),
        name=name,
    )(*inputs[:smem], *vmem_inputs)


VLIM = 10 * 1024 * 1024


def per_device(velocity, layer_widths, forward_prev, forward_now, adjoint_now, adjoint_later, source_cell, wavelet, receiver_cells, residuals):
    width, cells_y, cells_z = velocity.shape
    total_x = width * lax.axis_size("space")
    half = width // 2
    me = lax.axis_index("shot").astype(jnp.int32)
    place = lax.axis_index("space").astype(jnp.int32)
    scal = jnp.concatenate([layer_widths, (place * width)[None], source_cell[0], (place % 2)[None], me[None]])
    band = banded(cells_z)
    tz = jnp.asarray(np.concatenate([band, band], axis=0), BF16)
    ty = jnp.asarray(np.concatenate([banded(cells_y)] * 2, axis=1), BF16)
    sds = lambda n: jax.ShapeDtypeStruct((n, cells_y, cells_z), F32)
    count = lax.axis_size("space")
    swap_a = [(i, i ^ 1) for i in range(count)]
    swap_b = [(i, (i + (1 if i % 2 else -1)) % count) for i in range(count)]

    def exchange(to_a, to_b):
        from_b = lax.ppermute(to_b, "space", swap_b)
        return lax.ppermute(to_a, "space", swap_a), from_b

    fp, fn, an, al = forward_prev[0], forward_now[0], adjoint_now[0], adjoint_later[0]
    f_in = exchange(*pack(scal, [fn, fp, velocity], (half, 4, 4)))
    a_in = exchange(*pack(scal, [an, al], (half, 4)))
    receivers = residuals.shape[2]
    slots = receivers // LOAD
    loads, spots, table, left, rights, planes = call(
        functools.partial(receivers_kernel, 4, width + 8, cells_y, cells_z),
        [
            jax.ShapeDtypeStruct((1,), jnp.int32),
            jax.ShapeDtypeStruct((slots, LOAD), jnp.int32),
            jax.ShapeDtypeStruct((receivers, 128), F32),
            jax.ShapeDtypeStruct(((width + 8) * cells_y, LOAD), BF16),
            jax.ShapeDtypeStruct((residuals.shape[1], LOAD, 2 * cells_z), BF16),
            jax.ShapeDtypeStruct((3, 3, cells_y, cells_z), F32),
        ],
        [scal, receiver_cells[0], residuals[0]],
        [pltpu.VMEM((1, receivers), F32), pltpu.VMEM((128, receivers), BF16)],
        name="list_receivers",
        out_specs=[SMEM_SPEC] + [VMEM_SPEC] * 5,
    )
    tables = [("planes", planes), ("tz", tz), ("ty", ty)]

    def block(first, last, forward, level, arrived, own, extra, after):
        inputs = [("scal", scal), ("wave", wavelet) if forward else ("loads", loads), ("after", after)]
        inputs += [("from_a", arrived[0]), ("from_b", arrived[1]), ("own", own)] + extra + tables
        if not forward:
            inputs += [("spots", spots), ("table", table), ("left", left), ("rights", rights)]
        outs, out_names = [sds(width + 8), sds(width)], ["middle", "final"]
        if first and forward:
            outs.append(sds(width + 8))
            out_names.append("weight")
        if not last:
            outs += [sds(half)] * 2
            out_names += ["to_a", "to_b"]
            if forward:
                outs += [sds(width)] * 2
                out_names += ["curve_early", "curve_recent"]
            elif not first:
                outs.append(sds(width))
                out_names.append("image")
        elif forward:
            outs.append(sds(width))
            out_names.append("image")
        else:
            outs += [jax.ShapeDtypeStruct((8, half, 8, cells_z), F32)] * 4
            out_names += ["keep_low", "send_low", "keep_high", "send_high"]
        scratch, scratch_names = [pltpu.VMEM((width + 16, cells_y, cells_z), F32)], ["ext"]
        if first:
            scratch.append(pltpu.VMEM((width + 8, cells_y, cells_z), F32))
            scratch_names.append("prev")
        if last:
            outs.pop(0)
            out_names.pop(0)
            scratch.append(pltpu.VMEM((width + 8, cells_y, cells_z), F32))
            scratch_names.append("middle")
        if last and not forward:
            scratch.append(pltpu.VMEM((width, cells_y, cells_z), F32))
            scratch_names.append("image")
        out_specs = [VMEM_SPEC] * len(outs)
        outs.append(jax.ShapeDtypeStruct((1,), jnp.int32))
        out_names.append("turn")
        out_specs.append(SMEM_SPEC)
        names = [n for n, _ in inputs] + out_names + scratch_names
        got = call(
            functools.partial(block_kernel, first, last, forward, level, total_x, names),
            outs,
            [v for _, v in inputs],
            scratch,
            3,
            name=("forward" if forward else "adjoint") + "_block",
            out_specs=out_specs,
        )
        return dict(zip(out_names, got))

    def begin(forward, level, arrived, own, own_prev, extra, after):
        return block(True, False, forward, level, arrived, own, [("own_prev", own_prev)] + extra, after)

    def go_on(last, forward, level, arrived, before, after, more=()):
        extra = [("prev", before["middle"]), ("weight", weight)] + list(more)
        return block(False, last, forward, level, arrived, before["final"], extra, after)

    f0 = begin(True, 0, f_in, fn, fp, [("speeds", velocity)], loads)
    weight = f0["weight"]
    f_in = exchange(f0["to_a"], f0["to_b"])
    a0 = begin(False, 5, a_in, an, al, [("weight", weight)], f0["turn"])
    a_in = exchange(a0["to_a"], a0["to_b"])
    f1 = go_on(False, True, 2, f_in, f0, a0["turn"])
    f_in = exchange(f1["to_a"], f1["to_b"])
    curves = lambda block: [(n, block[n]) for n in ("curve_early", "curve_recent")]
    a1 = go_on(False, False, 3, a_in, a0, f1["turn"], curves(f1))
    a_in = exchange(a1["to_a"], a1["to_b"])
    fields = [("adjoint_early", a0["final"]), ("adjoint_recent", a0["middle"]), ("image_in", a1["image"])]
    f2 = go_on(True, True, 4, f_in, f1, a1["turn"], fields)
    a2 = go_on(True, False, 1, a_in, a1, f2["turn"], curves(f0) + [("image_in", f2["image"])])
    gradient = reduce_shots(me, a2["keep_low"], a2["send_low"], a2["keep_high"], a2["send_high"])
    return f2["final"][None], a2["final"][None], gradient


def flip(value, bit):
    return lax.ppermute(value, "shot", [(i, i ^ bit) for i in range(lax.axis_size("shot"))])


def reduce_shots(me, keep_a, send_a, keep_b, send_b):
    got_a, got_b = flip(send_a, 8), flip(send_b, 1)
    low_bit, top_bit = me & 1, me >> 3
    mid = (me >> 1) & 3
    half = keep_a.shape[1:]
    pick = lambda v, axis, i: lax.dynamic_index_in_dim(v, i, axis, keepdims=False)
    ka, ga = (v.reshape((4, 2) + half) for v in (keep_a, got_a))
    kb, gb = (v.reshape((2, 4) + half) for v in (keep_b, got_b))
    sa = pick(ka, 1, 1 - low_bit) + pick(ga, 1, 1 - low_bit)
    sb = pick(kb, 0, 1 - top_bit) + pick(gb, 0, 1 - top_bit)
    ra, rb = flip(sa, 1), flip(sb, 8)
    wa = pick(ka, 1, low_bit) + pick(ga, 1, low_bit) + ra
    wb = pick(kb, 0, top_bit) + pick(gb, 0, top_bit) + rb
    both = jnp.concatenate([wa, wb], axis=1)
    total = pick(both, 0, mid)
    for d in (1, 2, 3):
        total = total + flip(pick(both, 0, mid ^ d), 2 * d)
    return total


def solution(mesh):
    placed = (
        P("space", None, None),
        P(),
        P("shot", "space", None, None),
        P("shot", "space", None, None),
        P("shot", "space", None, None),
        P("shot", "space", None, None),
        P("shot", None),
        P("shot", None),
        P("shot", None, None),
        P("shot", None, None),
    )
    return jax.shard_map(
        per_device,
        mesh=mesh,
        in_specs=placed,
        out_specs=(P("shot", "space", None, None), P("shot", "space", None, None), P("space", "shot", None)),
        check_vma=False,
    )
```

```python
import functools

import jax
import jax.numpy as jnp
import numpy as np
from jax import lax
from jax.experimental import pallas as pl
from jax.experimental.pallas import tpu as pltpu
from jax.sharding import PartitionSpec as P

SCALE = 5040.0
CENTRE_Z, CENTRE_Y = -43008.0, -42.0
SIDE = (8064.0, -1008.0, 128.0, -9.0)
DT_OVER_H = 0.07
DAMPING_RATE = 0.15
SHOTS = 16
BATCH = 8
LOAD = 256
F32, BF16 = jnp.float32, jnp.bfloat16
VMEM = pltpu.VMEM
SMEM_SPEC = pl.BlockSpec(memory_space=pltpu.SMEM)
VMEM_SPEC = pl.BlockSpec(memory_space=pltpu.VMEM)


def banded(n, centre):
    offset = np.abs(np.arange(n)[:, None] - np.arange(n)[None, :])
    band = np.zeros((n, n), np.float32)
    for distance, coeff in enumerate(SIDE, start=1):
        band[offset == distance] = coeff
    band[offset == 0] = centre
    return band


def halves(value):
    high = value.astype(BF16)
    return high, (value - high.astype(F32)).astype(BF16)


def fill_planes(scal, planes, cells_y, cells_z):
    rows = lax.broadcasted_iota(jnp.int32, (cells_y, cells_z), 0)
    lanes = lax.broadcasted_iota(jnp.int32, (cells_y, cells_z), 1)
    absorb = (rows < scal[2]) | (rows >= cells_y - scal[3]) | (lanes < scal[4]) | (lanes >= cells_z - scal[5])
    damping = jnp.where(absorb, DAMPING_RATE, 0.0).astype(F32)
    full = jnp.full((cells_y, cells_z), DAMPING_RATE, F32)
    for kind, damp in enumerate((damping, full)):
        inverse = 1.0 / (1.0 + damp)
        planes[kind, 0] = inverse
        planes[kind, 1] = 2.0 * inverse
    planes[2] = jnp.zeros((2, cells_y, cells_z), F32)


def kind_of(scal, x, total_x):
    at = scal[6] + x
    outside = (at < 0) | (at >= total_x)
    absorbing = (at < scal[0]) | (at >= total_x - scal[1])
    return jnp.where(outside, 2, jnp.where(absorbing, 1, 0))


def right_of(table, load, level, cells_z):
    rows = pl.ds(pl.multiple_of(load * LOAD, LOAD), LOAD)
    lane = lax.broadcasted_iota(jnp.int32, (LOAD, cells_z), 1)
    at_z = lane == table[rows, 0:1].astype(jnp.int32)
    parts = [jnp.where(at_z, table[rows, 16 * p + level : 16 * p + level + 1], 0.0) for p in (1, 2)]
    return jnp.concatenate(parts, axis=1).astype(BF16)


def one_hot_rows(spots, load, first_layer, layers, cells_y):
    row = lax.broadcasted_iota(jnp.int32, (layers * cells_y, LOAD), 0) + first_layer * cells_y
    return jnp.where(row == spots[pl.ds(load, 1), :], 1.0, 0.0).astype(BF16)


def placed(left, right, cells_z):
    both = jnp.dot(left, right, preferred_element_type=F32)
    return both[:, :cells_z] + both[:, cells_z:]


def substep(scal, src, prev, prev_off, weight, weight_off, planes, tz, ty, inject, dest, low_x, layers, total_x, each=None, late=None):
    cells_y, cells_z = src.shape[1:]
    rows = 16
    if inject is not None:
        r, level, inject_off = inject

    def body(group, carry):
        base = group * BATCH
        high, low = halves(src[pl.ds(base + 4, BATCH)])
        side_by_side = jnp.concatenate([high, low], axis=2).reshape(BATCH * cells_y, 2 * cells_z)
        along = tz
        if inject is not None:
            first_row = pl.multiple_of((base + inject_off) * cells_y, cells_y)
            left = r["left"][pl.ds(first_row, BATCH * cells_y), :]
            side_by_side, along = jnp.concatenate([side_by_side, left], axis=1), r["rights"][level]
        along_z = jnp.dot(side_by_side, along, preferred_element_type=F32)
        if inject is not None:
            along_z = along_z[:, :cells_z] + along_z[:, cells_z:]
        stacked = jnp.concatenate(
            [jnp.concatenate([part[u] for u in range(BATCH)], axis=1) for part in (high, low)], axis=0
        )
        along_y = jnp.dot(ty, stacked, preferred_element_type=F32)
        partial = [
            along_z[u * cells_y : (u + 1) * cells_y] + along_y[:, u * cells_z : (u + 1) * cells_z]
            for u in range(BATCH)
        ]
        kinds = [kind_of(scal, low_x + base + u, total_x) for u in range(BATCH)]
        for chunk in range(cells_y // rows):
            at = slice(chunk * rows, (chunk + 1) * rows)
            column = [src[base + i, at, :] for i in range(BATCH + 8)]
            for u in range(BATCH):
                centre = column[u + 4]
                total = partial[u][at, :]
                for distance, coeff in enumerate(SIDE, start=1):
                    total = total + coeff * (column[u + 4 - distance] + column[u + 4 + distance])
                kind = kinds[u]
                before = prev[base + u + prev_off, at, :]
                new = weight[base + u + weight_off, at, :] * total + (planes[kind, 1, at, :] * (centre - before) + before)
                dest[base + u, at, :] = new
                if each is not None:
                    each(base + u, at, new, centre, before)
        return carry

    lax.fori_loop(0, layers // BATCH, body, 0)
    if inject is not None:

        def another_load(load, carry):
            more = right_of(r["table"], load, level, cells_z)

            def one_layer(x, c):
                left = one_hot_rows(r["spots"], load, x + inject_off, 1, cells_y)
                term = weight[x + weight_off] * placed(left, more, cells_z)
                dest[x] = dest[x] + term
                if late is not None:
                    late(x, slice(None), term)
                return c

            return lax.fori_loop(0, layers, one_layer, carry)

        lax.fori_loop(1, r["loads"][0], another_load, 0)


def add_source(scal, amplitude, weight, weight_off, dest, low_x, layers, late=None):
    x = scal[7] - scal[6] - low_x

    @pl.when((x >= 0) & (x < layers))
    def _():
        row = pl.ds(scal[8], 1)
        lane = lax.broadcasted_iota(jnp.int32, (1, dest.shape[2]), 1)
        gain = weight[x + weight_off, row, :] * (SCALE * amplitude)
        term = jnp.where(lane == scal[9], gain, 0.0)
        dest[x, row, :] = dest[x, row, :] + term
        if late is not None:
            late(x, row, term)


def block_kernel(first, last, forward, level, total_x, names, *refs):
    r = dict(zip(names, refs))
    scal, planes, ext, weight = r["scal"], r["planes"], r["ext"], r["weight"]
    width = r["own"].shape[0]
    half = width // 2
    odd = scal[10]
    r["turn"][0] = r["after"][0]
    low_edge, high_edge = scal[6] == 0, scal[6] + width == total_x
    at_edge = low_edge | high_edge
    halo_a, halo_b = pl.ds((1 - odd) * (8 + width), 8), pl.ds(odd * (8 + width), 8)
    ext[halo_a] = r["from_a"][:8]
    ext[halo_b] = jnp.where(at_edge, 0.0, r["from_b"][:8])
    ext[8 : 8 + width] = r["own"][...]
    if first:
        prev = r["prev"]
        thin_a, thin_b = pl.ds((1 - odd) * (4 + width), 4), pl.ds(odd * (4 + width), 4)
        prev[thin_a] = r["from_a"][8:12]
        prev[thin_b] = jnp.where(at_edge, 0.0, r["from_b"][8:12])
        prev[4 : 4 + width] = r["own_prev"][...]
        if forward:
            gain = DT_OVER_H * DT_OVER_H / SCALE
            weight[thin_a] = gain * r["from_a"][12:] * r["from_a"][12:]
            weight[thin_b] = gain * r["from_b"][12:] * r["from_b"][12:]
            weight[4 : 4 + width] = gain * r["speeds"][...] * r["speeds"][...]

            def damp(x, carry):
                weight[x] = planes[kind_of(scal, x - 4, total_x), 0] * weight[x]
                return carry

            lax.fori_loop(0, width + 8, damp, 0)
    else:
        prev = r["prev"]
    tz, ty = r["tz"][...], r["ty"][...]
    middle, final = r["middle"], r["final"]
    inject = (lambda n, off: None) if forward else (lambda n, off: (r, n, off))
    substep(scal, ext, prev, 0, weight, 0, planes, tz, ty, inject(level, 0), middle, -4, width + 8, total_x)
    if forward:
        add_source(scal, r["wave"][0, level], weight, 0, middle, -4, width + 8)

    each = late = None
    image = r.get("image")
    if forward:

        def curvatures(x, at, new, centre, before):
            return centre - 2.0 * before + prev[x + 4, at, :], new - 2.0 * centre + before

        if last:

            def each(x, at, *states):
                early, recent = curvatures(x, at, *states)
                terms = r["adjoint_early"][x, at, :] * early + r["adjoint_recent"][x + 4, at, :] * recent
                image[x, at, :] = r["image_in"][x, at, :] + terms

            def late(x, at, term):
                image[x, at, :] = image[x, at, :] + r["adjoint_recent"][x + 4, at, :] * term

        else:

            def each(x, at, *states):
                r["curve_early"][x, at, :], r["curve_recent"][x, at, :] = curvatures(x, at, *states)

            def late(x, at, term):
                r["curve_recent"][x, at, :] = r["curve_recent"][x, at, :] + term

    elif not first:

        def each(x, at, new, centre, before):
            terms = centre * r["curve_recent"][x, at, :] + new * r["curve_early"][x, at, :]
            image[x, at, :] = r["image_in"][x, at, :] + terms if last else terms

        def late(x, at, term):
            image[x, at, :] = image[x, at, :] + term * r["curve_early"][x, at, :]

    substep(scal, middle, ext, 8, weight, 4, planes, tz, ty, inject(level - 1, 4), final, 0, width, total_x, each, late)
    if forward:
        add_source(scal, r["wave"][0, level + 1], weight, 4, final, 0, width, late)
    if not last:
        r["to_a"][...] = final[pl.ds((1 - odd) * half, half)]
        r["to_b"][...] = final[pl.ds(odd * half, half)]
    elif not forward:
        low_bit, top_bit = scal[11] & 1, scal[11] >> 3
        shares = [[r["keep_low"], r["send_low"]], [r["keep_high"], r["send_high"]]]
        share = 1.0 / SHOTS

        def one_chunk(j, carry):
            for which in range(2):
                for upper, chunk in enumerate(((top_bit ^ which) * 8 + j, j * 2 + (low_bit ^ which))):
                    at = pl.ds(pl.multiple_of(chunk * 8, 8), 8)
                    shares[upper][which][j] = share * image[upper * half : (upper + 1) * half, at, :]
            return carry

        lax.fori_loop(0, 8, one_chunk, 0)


def receivers_kernel(low_off, layers, cells_y, cells_z, scal, cells, values, tz, loads, spots, table, left, rights, planes, counts, entries):
    fill_planes(scal, planes, cells_y, cells_z)
    steps, receivers = values.shape
    groups = receivers // 128
    x = cells[0:1, :] - scal[6] + low_off
    inside = (x >= 0) & (x < layers)
    key = jnp.where(inside, x * cells_y + cells[1:2, :], -1)
    flag = jnp.where(inside, 1.0, 0.0).astype(F32)
    flag_rows = jnp.concatenate([flag[:, g * 128 : (g + 1) * 128] for g in range(groups)], axis=0)
    r0 = lax.broadcasted_iota(jnp.int32, (128, 128), 0)
    r1 = lax.broadcasted_iota(jnp.int32, (128, 128), 1)
    upper = jnp.where(r0 <= r1, 1.0, 0.0).astype(BF16)
    within = jnp.dot(flag_rows.astype(BF16), upper, preferred_element_type=F32)
    g0 = lax.broadcasted_iota(jnp.int32, (groups, groups), 0)
    g1 = lax.broadcasted_iota(jnp.int32, (groups, groups), 1)
    before = jnp.where(g1 < g0, 1.0, 0.0).astype(BF16)
    totals = jnp.broadcast_to(within[:, 127:128], (groups, 128)).astype(BF16)
    rank = within - flag_rows + jnp.dot(before, totals, preferred_element_type=F32)
    rank = jnp.where(flag_rows > 0.0, rank, -1.0)
    for g in range(groups):
        counts[0:1, g * 128 : (g + 1) * 128] = rank[g : g + 1, :]
    number = jnp.sum(flag).astype(jnp.int32)
    filled_loads = jnp.maximum((number + LOAD - 1) // LOAD, 1)
    loads[0] = filled_loads
    high_key = key // 128
    parts = [cells[2:3, :].astype(F32), high_key.astype(F32), (key - high_key * 128).astype(F32)]
    entries[0:16] = jnp.concatenate(parts + [jnp.zeros((13, receivers), F32)], axis=0).astype(BF16)
    scaled = values[...] * SCALE
    high = scaled.astype(BF16)
    rest = (scaled - high.astype(F32)).astype(BF16)
    pad = jnp.zeros((16 - steps, receivers), BF16)
    entries[16:32] = jnp.concatenate([high, pad], axis=0)
    entries[32:48] = jnp.concatenate([rest, pad], axis=0)
    entries[48:] = jnp.zeros((entries.shape[0] - 48, receivers), BF16)

    def one_load(load, carry):
        slot = lax.broadcasted_iota(jnp.int32, (LOAD, receivers), 0) + load * LOAD
        pick = jnp.where(slot == counts[0:1, :].astype(jnp.int32), 1.0, 0.0).astype(BF16)
        nt = (((1,), (1,)), ((), ()))
        picked = lax.dot_general(entries[0:16], pick, nt, preferred_element_type=F32)
        column = lax.dot_general(pick, entries[...], nt, preferred_element_type=F32)
        filled = (lax.broadcasted_iota(jnp.int32, (1, LOAD), 1) + load * LOAD) < number
        spot = (picked[1:2] * 128.0 + picked[2:3]).astype(jnp.int32)
        spots[pl.ds(load, 1), :] = jnp.where(filled, spot, -1)
        table[pl.ds(pl.multiple_of(load * LOAD, LOAD), LOAD), :] = column
        return carry

    lax.fori_loop(0, filled_loads, one_load, 0)
    for group in range(layers // BATCH):
        at = slice(group * BATCH * cells_y, (group + 1) * BATCH * cells_y)
        left[at, :] = one_hot_rows(spots, 0, group * BATCH, BATCH, cells_y)
    for step in range(steps):
        right = right_of(table, 0, step, cells_z)
        beside = jnp.concatenate([tz[...], jnp.zeros(tz.shape, BF16)], axis=1)
        rights[step] = jnp.concatenate([beside, right], axis=0)


def pack_kernel(plan, width, count, scal, *refs):
    inputs, outs, sems = refs[:count], refs[count:-1], refs[-1]
    copies = []
    for out, at_high in zip(outs, (1 - scal[10], scal[10])):
        at = 0
        for array, layers in zip(inputs, plan):
            source = array.at[pl.ds(at_high * (width - layers), layers)]
            copies.append(pltpu.make_async_copy(source, out.at[pl.ds(at, layers)], sems.at[len(copies)]))
            at += layers
    for copy in copies:
        copy.start()
    for copy in copies:
        copy.wait()


def pack(scal, arrays, plan):
    out = jax.ShapeDtypeStruct((sum(plan),) + arrays[0].shape[1:], F32)
    return pl.pallas_call(
        functools.partial(pack_kernel, plan, arrays[0].shape[0], len(arrays)),
        out_shape=[out] * 2,
        in_specs=[SMEM_SPEC] + [pl.BlockSpec(memory_space=pltpu.HBM)] * len(arrays),
        out_specs=[VMEM_SPEC] * 2,
        scratch_shapes=[pltpu.SemaphoreType.DMA((2 * len(plan),))],
        compiler_params=pltpu.CompilerParams(vmem_limit_bytes=VLIM),
        cost_estimate=pl.CostEstimate(flops=0, bytes_accessed=4 << 20, transcendentals=0),
        name="pack",
    )(scal, *[pltpu.with_memory_space_constraint(x, pltpu.HBM) for x in arrays])


def call(kernel, out_shapes, inputs, scratch=(), smem=1, cost=(0, 14 << 20), name=None, out_specs=None):
    vmem_inputs = [x for x in inputs[smem:]]
    return pl.pallas_call(
        kernel,
        out_shape=out_shapes,
        in_specs=[SMEM_SPEC] * smem + [VMEM_SPEC] * len(vmem_inputs),
        out_specs=out_specs or [VMEM_SPEC] * len(out_shapes),
        scratch_shapes=list(scratch),
        compiler_params=pltpu.CompilerParams(vmem_limit_bytes=VLIM),
        cost_estimate=pl.CostEstimate(flops=cost[0], bytes_accessed=cost[1], transcendentals=0),
        name=name,
    )(*inputs[:smem], *vmem_inputs)


VLIM = 10 * 1024 * 1024


def per_device(velocity, layer_widths, forward_prev, forward_now, adjoint_now, adjoint_later, source_cell, wavelet, receiver_cells, residuals):
    width, cells_y, cells_z = velocity.shape
    total_x = width * lax.axis_size("space")
    half = width // 2
    me = lax.axis_index("shot").astype(jnp.int32)
    place = lax.axis_index("space").astype(jnp.int32)
    scal = jnp.concatenate([layer_widths, (place * width)[None], source_cell[0], (place % 2)[None], me[None]])
    band = banded(cells_z, CENTRE_Z)
    tz = jnp.asarray(np.concatenate([band, band], axis=0), BF16)
    ty = jnp.asarray(np.concatenate([banded(cells_y, CENTRE_Y)] * 2, axis=1), BF16)
    sds = lambda n: jax.ShapeDtypeStruct((n, cells_y, cells_z), F32)
    count = lax.axis_size("space")
    swap_a = [(i, i ^ 1) for i in range(count)]
    swap_b = [(i, (i + (1 if i % 2 else -1)) % count) for i in range(count)]

    def exchange(to_a, to_b):
        from_b = lax.ppermute(to_b, "space", swap_b)
        return lax.ppermute(to_a, "space", swap_a), from_b

    fp, fn, an, al = forward_prev[0], forward_now[0], adjoint_now[0], adjoint_later[0]
    f_in = exchange(*pack(scal, [fn, fp, velocity], (half, 4, 4)))
    a_in = exchange(*pack(scal, [an, al], (half, 4)))
    receivers = residuals.shape[2]
    slots = receivers // LOAD
    loads, spots, table, left, rights, planes = call(
        functools.partial(receivers_kernel, 4, width + 8, cells_y, cells_z),
        [
            jax.ShapeDtypeStruct((1,), jnp.int32),
            jax.ShapeDtypeStruct((slots, LOAD), jnp.int32),
            jax.ShapeDtypeStruct((receivers, 128), F32),
            jax.ShapeDtypeStruct(((width + 8) * cells_y, LOAD), BF16),
            jax.ShapeDtypeStruct((residuals.shape[1], 2 * cells_z + LOAD, 2 * cells_z), BF16),
            jax.ShapeDtypeStruct((3, 2, cells_y, cells_z), F32),
        ],
        [scal, receiver_cells[0], residuals[0], tz],
        [pltpu.VMEM((1, receivers), F32), pltpu.VMEM((128, receivers), BF16)],
        name="list_receivers",
        out_specs=[SMEM_SPEC] + [VMEM_SPEC] * 5,
    )
    tables = [("planes", planes), ("tz", tz), ("ty", ty)]

    def block(first, last, forward, level, arrived, own, extra, after):
        inputs = [("scal", scal), ("wave", wavelet) if forward else ("loads", loads), ("after", after)]
        inputs += [("from_a", arrived[0]), ("from_b", arrived[1]), ("own", own)] + extra + tables
        if not forward:
            inputs += [("spots", spots), ("table", table), ("left", left), ("rights", rights)]
        outs, out_names = [sds(width + 8), sds(width)], ["middle", "final"]
        if first and forward:
            outs.append(sds(width + 8))
            out_names.append("weight")
        if not last:
            outs += [sds(half)] * 2
            out_names += ["to_a", "to_b"]
            if forward:
                outs += [sds(width)] * 2
                out_names += ["curve_early", "curve_recent"]
            elif not first:
                outs.append(sds(width))
                out_names.append("image")
        elif forward:
            outs.append(sds(width))
            out_names.append("image")
        else:
            outs += [jax.ShapeDtypeStruct((8, half, 8, cells_z), F32)] * 4
            out_names += ["keep_low", "send_low", "keep_high", "send_high"]
        scratch, scratch_names = [pltpu.VMEM((width + 16, cells_y, cells_z), F32)], ["ext"]
        if first:
            scratch.append(pltpu.VMEM((width + 8, cells_y, cells_z), F32))
            scratch_names.append("prev")
        if last:
            outs.pop(0)
            out_names.pop(0)
            scratch.append(pltpu.VMEM((width + 8, cells_y, cells_z), F32))
            scratch_names.append("middle")
        if last and not forward:
            scratch.append(pltpu.VMEM((width, cells_y, cells_z), F32))
            scratch_names.append("image")
        out_specs = [VMEM_SPEC] * len(outs)
        outs.append(jax.ShapeDtypeStruct((1,), jnp.int32))
        out_names.append("turn")
        out_specs.append(SMEM_SPEC)
        names = [n for n, _ in inputs] + out_names + scratch_names
        got = call(
            functools.partial(block_kernel, first, last, forward, level, total_x, names),
            outs,
            [v for _, v in inputs],
            scratch,
            3,
            name=("forward" if forward else "adjoint") + "_block",
            out_specs=out_specs,
        )
        return dict(zip(out_names, got))

    def begin(forward, level, arrived, own, own_prev, extra, after):
        return block(True, False, forward, level, arrived, own, [("own_prev", own_prev)] + extra, after)

    def go_on(last, forward, level, arrived, before, after, more=()):
        extra = [("prev", before["middle"]), ("weight", weight)] + list(more)
        return block(False, last, forward, level, arrived, before["final"], extra, after)

    f0 = begin(True, 0, f_in, fn, fp, [("speeds", velocity)], loads)
    weight = f0["weight"]
    f_in = exchange(f0["to_a"], f0["to_b"])
    a0 = begin(False, 5, a_in, an, al, [("weight", weight)], f0["turn"])
    a_in = exchange(a0["to_a"], a0["to_b"])
    f1 = go_on(False, True, 2, f_in, f0, a0["turn"])
    f_in = exchange(f1["to_a"], f1["to_b"])
    curves = lambda block: [(n, block[n]) for n in ("curve_early", "curve_recent")]
    a1 = go_on(False, False, 3, a_in, a0, f1["turn"], curves(f1))
    a_in = exchange(a1["to_a"], a1["to_b"])
    fields = [("adjoint_early", a0["final"]), ("adjoint_recent", a0["middle"]), ("image_in", a1["image"])]
    f2 = go_on(True, True, 4, f_in, f1, a1["turn"], fields)
    a2 = go_on(True, False, 1, a_in, a1, f2["turn"], curves(f0) + [("image_in", f2["image"])])
    gradient = reduce_shots(me, a2["keep_low"], a2["send_low"], a2["keep_high"], a2["send_high"])
    return f2["final"][None], a2["final"][None], gradient


def flip(value, bit):
    return lax.ppermute(value, "shot", [(i, i ^ bit) for i in range(lax.axis_size("shot"))])


def reduce_shots(me, keep_a, send_a, keep_b, send_b):
    got_a, got_b = flip(send_a, 8), flip(send_b, 1)
    low_bit, top_bit = me & 1, me >> 3
    mid = (me >> 1) & 3
    half = keep_a.shape[1:]
    pick = lambda v, axis, i: lax.dynamic_index_in_dim(v, i, axis, keepdims=False)
    ka, ga = (v.reshape((4, 2) + half) for v in (keep_a, got_a))
    kb, gb = (v.reshape((2, 4) + half) for v in (keep_b, got_b))
    sa = pick(ka, 1, 1 - low_bit) + pick(ga, 1, 1 - low_bit)
    sb = pick(kb, 0, 1 - top_bit) + pick(gb, 0, 1 - top_bit)
    ra, rb = flip(sa, 1), flip(sb, 8)
    wa = pick(ka, 1, low_bit) + pick(ga, 1, low_bit) + ra
    wb = pick(kb, 0, top_bit) + pick(gb, 0, top_bit) + rb
    both = jnp.concatenate([wa, wb], axis=1)
    total = pick(both, 0, mid)
    for d in (1, 2, 3):
        total = total + flip(pick(both, 0, mid ^ d), 2 * d)
    return total


def solution(mesh):
    placed = (
        P("space", None, None),
        P(),
        P("shot", "space", None, None),
        P("shot", "space", None, None),
        P("shot", "space", None, None),
        P("shot", "space", None, None),
        P("shot", None),
        P("shot", None),
        P("shot", None, None),
        P("shot", None, None),
    )
    return jax.shard_map(
        per_device,
        mesh=mesh,
        in_specs=placed,
        out_specs=(P("shot", "space", None, None), P("shot", "space", None, None), P("space", "shot", None)),
        check_vma=False,
    )
```
